32 devices in a mesh: grp: 2 (over x), seq: 16 (over z, y, core).
Axes of the slice: x: 2, y: 2, z: 4, core: 2. Of those that a mesh axis runs over, the one named last changes fastest.
Arguments:
- queries: bfloat16 [16384, 1536], P(('grp', 'seq')), parts along dimension 0, may hold values from -26 to 26
- keys_values: bfloat16 [2, 16384, 1536], P(None, ('grp', 'seq')), parts along dimension 1, may hold values from -26 to 26
- segment_ids: int32 [16384], P('grp'), parts along dimension 0, may hold values from 0 to 31, never falling along the last dimension, each value on 1 to 512 neighbouring positions
- route_shard: int32 [16384, 1], P(('grp', 'seq')), parts along dimension 0, may hold values from 0 to 15; in each aligned block of 512 rows (0 to 511, 512 to 1023, ...) at most 64 rows name the same one
- route_slot: int32 [16384], P(('grp', 'seq')), parts along dimension 0, may hold values from 0 to 511
- control_proj: bfloat16 [1536, 3072], replicated, may hold values from -0.15625 to 0.15625
- base_hidden: bfloat16 [16384, 3072], P(('grp', 'seq')), parts along dimension 0, may hold values from -6 to 6
- cotangent: bfloat16 [16384, 3072], P(('grp', 'seq')), parts along dimension 0, may hold values from -1.25 to 1.25
Outputs:
- mixed_hidden: bfloat16 [16384, 3072], P(('grp', 'seq')), parts along dimension 0
- proj_grad: float32 [3072, 3072], P(('grp', 'seq')), parts along dimension 0
The draws below stay inside these ranges and needn't reach their ends.
There are 2 independent parts, one for each index of `grp`. The reference program is written for one: setup_inputs(seed, part) draws one part's arguments, and reference() takes and returns one part's arrays. A program takes and returns all parts, laid end to end along the dimension named above; an argument that names none is the same for every part. Nothing has to cross between parts.
Inputs may be any that keep to these rules, and one draw needn't show every extreme that they name: `segment_ids`: segment numbers never fall along the sequence; each image spans 1 to 512 tokens, one exactly 512. `route_shard`: of the 512 rows of one device, at most 64 name the same base shard; in every draw some device sends exactly 64 rows to one shard.
All inputs are finite; a program needn't handle non-finite values.
Results may differ from the reference program's by a relative error of at most 0.008.
Values may be sent and summed in bfloat16 or wider, within the bound.
No kernel may reach another device: no remote copies, remote signals or barrier semaphores. Data moves between devices by JAX's collectives and lax.ppermute only.
A program may use at most 192 MiB of HBM per device.

```python
import math
import jax
import jax.numpy as jnp
import numpy as np
from jax import lax

D = 3072
HEAD = 128
HEADS = 12
SEG_MAX = 512
TOK_DEV = 512
HW = 1536
TOKENS = 8192
CAP = 64
SEGS = 32
N_SEQ = 16


def fresh_field(key, salt):
    raw = jax.random.normal(jax.random.fold_in(key, salt), (TOKENS, HEADS * HEAD), jnp.float32)
    return jnp.clip(raw, -4.0, 4.0)


def draw_queries(key, part):
    field = fresh_field(key, 21)
    return field.astype(jnp.bfloat16)


def draw_keys_values(key, part):
    key_field = fresh_field(key, 31)
    value_field = fresh_field(key, 41)
    return jnp.stack([key_field, value_field]).astype(jnp.bfloat16)


def plant(values, stream_key, least, high):
    place = [jax.random.randint(jax.random.fold_in(stream_key, axis), (), 0, length) for axis, length in enumerate(values.shape)]
    widest = values.shape.index(max(values.shape))
    beside = place[:widest] + [(place[widest] + 1) % values.shape[widest]] + place[widest + 1:]
    return values.at[tuple(place)].set(least).at[tuple(beside)].set(high)


def steps_of(own_key, shape, split, least, largest):
    level, own = 1.0, jax.random.fold_in(own_key, 6)
    for dim, blocks in split:
        draws = jnp.exp(jax.random.uniform(jax.random.fold_in(own, dim), (blocks,), jnp.float32, least / len(split), largest / len(split)))
        level = level * jnp.repeat(draws, shape[dim] // blocks).reshape([-1 if axis == dim else 1 for axis in range(len(shape))])
    return level


def split_up(number_of, total, reach, skew):
    portions = [(1 << 20) // math.isqrt(rank ** skew) + 1 for rank in range(2, number_of + 1)]
    rest, counts = total - reach - (number_of - 1), [1] * (number_of - 1)
    while rest > 0:
        movable = [i for i in range(number_of - 1) if counts[i] < reach]
        whole, left = sum([portions[i] for i in movable]), rest
        for i in movable:
            extra = min(reach - counts[i], max(1, left * portions[i] // whole), rest)
            counts[i] = counts[i] + extra
            rest = rest - extra
    return np.array([reach] + counts)


def ragged_sizes(own_key, amount, total, bound, lean):
    if amount == 2:
        one = jax.random.randint(own_key, (), max(1, total - bound), min(bound, total - 1) + 1)
        return jnp.stack([one, total - one])
    sizes = jnp.asarray(split_up(amount, total, bound, lean), jnp.int32)
    pairs = (amount - 1) // 2
    giver, sink = sizes[1:1 + 2 * pairs:2], sizes[2:2 + 2 * pairs:2]
    margin = jnp.minimum(giver - 1, bound - sink)
    shifted = jax.random.randint(jax.random.fold_in(own_key, 1), (pairs,), 0, 1 << 20) % (margin + 1)
    sizes = sizes.at[1:1 + 2 * pairs:2].set(giver - shifted).at[2:2 + 2 * pairs:2].set(sink + shifted)
    return sizes[jax.random.permutation(jax.random.fold_in(own_key, 2), amount)]


def routed_block(key, own, number, rows, number_of, top, reach, lean):
    ranking = jax.random.permutation(key, number_of)
    packed, ordinary = load_shares(number_of, rows * top, reach, lean, True), load_shares(number_of, rows * top, reach, lean, False)
    places = jnp.arange(number_of)

    def named(lengths, offset_by):
        used = int((lengths > 0).sum())
        fixed = max(1, used // 4)
        passed = fixed + (places - fixed + offset_by * (used - fixed)) % max(1, number_of - fixed)
        return jnp.zeros((number_of,), jnp.int32).at[ranking[jnp.where(places < fixed, places, passed)]].set(jnp.asarray(lengths, jnp.int32))

    lengths = jnp.where(number % 4 == 0, named(packed, number // 4), named(ordinary, number - number // 4 - 1))
    mixed = jax.random.permutation(jax.random.fold_in(own, 3), number_of)
    giver, taker = mixed[0:number_of // 2 * 2:2], mixed[1:number_of // 2 * 2:2]
    margin = jnp.minimum(lengths[giver] - 1, reach - lengths[taker]) // 2
    margin = jnp.where((giver == ranking[0]) | (taker == ranking[0]) | (lengths[taker] == 0), 0, jnp.maximum(margin, 0))
    passed = jax.random.randint(jax.random.fold_in(own, 4), (number_of // 2,), 0, 1 << 20) % (margin + 1)
    lengths = lengths.at[giver].add(-passed).at[taker].add(passed)
    items = jnp.searchsorted(jnp.cumsum(lengths), jnp.arange(rows * top), side="right").astype(jnp.int32)
    table = items.reshape(top, rows).T
    table = table[jax.random.permutation(jax.random.fold_in(own, 1), rows)]
    offset_by = jax.random.randint(jax.random.fold_in(own, 2), (rows, 1), 0, top)
    return jnp.take_along_axis(table, (jnp.arange(top)[None, :] + offset_by) % top, axis=1)


def load_shares(number_of, total, limit, lean, full):
    weights = [(1 << 20) // math.isqrt(grade ** lean) + 1 for grade in range(1, number_of + 1)]
    largest = limit if full else min(limit, max(-(-total // number_of), total * weights[0] // sum(weights)))
    least = 1 if total - largest >= number_of - 1 else 0
    holding, rest = [largest] + [least] * (number_of - 1), total - largest - least * (number_of - 1)
    while rest > 0:
        free = [i for i in range(1, number_of) if holding[i] < largest] or [i for i in range(1, number_of) if holding[i] < limit]
        whole, budget = sum([weights[i] for i in free]), rest
        for i in free:
            extra = min(limit - holding[i], max(1, budget * weights[i] // whole), rest)
            holding[i] = holding[i] + extra
            rest = rest - extra
    return np.array(holding)


def noise(rng, dims, deviation, most, pieces=(), held_as=jnp.bfloat16):
    entries = jax.random.normal(rng, dims, jnp.float32) * deviation
    if len(pieces) > 0:
        entries = steps_of(rng, dims, pieces, -0.22, 0.18) * entries
    return jnp.clip(entries, min=-most, max=most).astype(held_as)


def setup_inputs(seed: int = 0, part: int = 0) -> dict:
    key_list = jax.random.split(jax.random.key(seed), 9)
    part_splits = jax.random.split(jax.random.fold_in(key_list[8], part), 9)
    queries = draw_queries(jax.random.fold_in(jax.random.fold_in(key_list[8], part), 71), part)
    keys_values = draw_keys_values(jax.random.fold_in(jax.random.fold_in(key_list[8], part), 71), part)
    segment_ids = jnp.searchsorted(jnp.cumsum(ragged_sizes(part_splits[2], SEGS, TOKENS, SEG_MAX, 1)), jnp.arange(TOKENS), side="right").astype(jnp.int32)
    route_shard_keys = jax.random.split(jax.random.fold_in(part_splits[3], 1), TOKENS // TOK_DEV)
    route_shard_turns = jax.random.permutation(jax.random.fold_in(part_splits[3], 3), TOKENS // TOK_DEV)
    route_shard = jax.vmap(lambda own, number: routed_block(jax.random.fold_in(part_splits[3], 2), own, number, TOK_DEV, N_SEQ, 1, CAP, 2))(route_shard_keys, route_shard_turns).reshape((TOKENS, 1))
    route_slot = plant(jax.random.randint(part_splits[4], (TOKENS,), 0, TOK_DEV), jax.random.fold_in(part_splits[4], 1), 0, TOK_DEV - 1).astype(jnp.int32)
    control_proj = noise(key_list[5], (HW, D), HW ** -0.5, 0.15625)
    base_hidden = noise(part_splits[6], (TOKENS, D), 1.0, 6.0, ((0, 16),))
    cotangent = noise(part_splits[7], (TOKENS, D), (8 * TOKENS ** -0.5), 1.25, ((0, 16),))
    return {"queries": queries, "keys_values": keys_values, "segment_ids": segment_ids, "route_shard": route_shard, "route_slot": route_slot, "control_proj": control_proj, "base_hidden": base_hidden, "cotangent": cotangent}


def attend_block(query_rows, near_pairs, query_seg, key_seg):
    row_count = query_rows.shape[0]
    query_heads = query_rows.reshape(row_count, HEADS, HEAD).astype(jnp.float32)
    key_heads = near_pairs[0].reshape(-1, HEADS, HEAD).astype(jnp.float32)
    value_heads = near_pairs[1].reshape(-1, HEADS, HEAD).astype(jnp.float32)
    scores = jnp.einsum("qhd,khd->hqk", query_heads, key_heads) * (HEAD ** -0.5)
    keep_mask = (query_seg[:, None] == key_seg[None, :])[None]
    scores = jnp.where(keep_mask, scores, -1e30)
    row_peak = jnp.max(scores, axis=2, keepdims=True)
    exp_scores = jnp.where(keep_mask, jnp.exp(scores - row_peak), 0.0)
    attn_weights = (exp_scores / jnp.sum(exp_scores, axis=2, keepdims=True)).astype(jnp.bfloat16)
    result = jnp.einsum("hqk,khd->qhd", attn_weights.astype(jnp.float32), value_heads)
    return result.reshape(row_count, HEADS * HEAD).astype(jnp.bfloat16)


def reference(queries, keys_values, segment_ids, route_shard, route_slot, control_proj, base_hidden, cotangent):
    padded_pairs = jnp.pad(keys_values, ((0, 0), (SEG_MAX, SEG_MAX), (0, 0)))
    padded_seg = jnp.pad(segment_ids, (SEG_MAX, SEG_MAX), constant_values=-1)

    def one_block(block_index):
        first_row = (block_index * TOK_DEV).astype(jnp.int32)
        query_rows = lax.dynamic_slice_in_dim(queries, first_row, TOK_DEV, 0)
        near_pairs = lax.dynamic_slice_in_dim(padded_pairs, first_row, TOK_DEV + 2 * SEG_MAX, 1)
        query_seg = lax.dynamic_slice_in_dim(segment_ids, first_row, TOK_DEV, 0)
        key_seg = lax.dynamic_slice_in_dim(padded_seg, first_row, TOK_DEV + 2 * SEG_MAX, 0)
        return attend_block(query_rows, near_pairs, query_seg, key_seg)

    attended = lax.map(one_block, jnp.arange(N_SEQ, dtype=jnp.int32)).reshape(TOKENS, HEADS * HEAD)
    residual = jnp.dot(attended, control_proj, preferred_element_type=jnp.float32).astype(jnp.bfloat16)
    base_row = (route_shard[:, 0] * TOK_DEV + route_slot).astype(jnp.int32)
    added = jax.ops.segment_sum(residual.astype(jnp.float32), base_row, num_segments=TOKENS)
    mixed_hidden = (base_hidden.astype(jnp.float32) + added).astype(jnp.bfloat16)
    returned = cotangent[base_row]

    def add_partial(running, block_index):
        first_row = (block_index * TOK_DEV).astype(jnp.int32)
        columns = lax.dynamic_slice_in_dim(attended, first_row, TOK_DEV, 0)
        grad_block = lax.dynamic_slice_in_dim(returned, first_row, TOK_DEV, 0)
        partial_term = jnp.dot(columns.T, grad_block, preferred_element_type=jnp.float32)
        return running + partial_term, None

    start_value = jnp.zeros((HEADS * HEAD, D), jnp.float32)
    proj_grad, unused = lax.scan(add_partial, start_value, jnp.arange(N_SEQ, dtype=jnp.int32))
    return mixed_hidden, proj_grad
```

```python
import functools
import math

import jax
import jax.numpy as jnp
from jax import lax
from jax.experimental import pallas as pl
from jax.experimental.pallas import tpu as pltpu
from jax.sharding import PartitionSpec as P

HEAD = 128
SEG_MAX = 512
QUERY_BLOCK = 256
KEY_BLOCK = 256
HEADS_PER_STEP = 3
HEAD_CHUNKS = 1
GRAD_CHUNKS = 2
MASKED = -1e30
EXP2_SCALE = HEAD ** (-0.5) * math.log2(math.e)


def attend_kernel(
    bounds, query_ref, before_ref, own_ref, after_ref, query_seg_ref, key_seg_ref, place_ref,
    out_ref, attended_ref,
):
    row_count = query_ref.shape[0]
    for block in range(row_count // QUERY_BLOCK):
        rows = slice(block * QUERY_BLOCK, (block + 1) * QUERY_BLOCK)
        query_seg = query_seg_ref[:, rows]
        heads = [slice(h * HEAD, (h + 1) * HEAD) for h in range(HEADS_PER_STEP)]
        queries = [query_ref[rows, head] for head in heads]

        def step(pair_ref, first_key, key_block, state):
            offset = pl.multiple_of(key_block * KEY_BLOCK, KEY_BLOCK)
            key_seg = key_seg_ref[pl.ds(first_key + offset, KEY_BLOCK), :]
            keep = key_seg == query_seg
            result = []
            for head, query, (peak, total, summed) in zip(heads, queries, state):
                keys = pair_ref[0, pl.ds(offset, KEY_BLOCK), head]
                values = pair_ref[1, pl.ds(offset, KEY_BLOCK), head]
                scores = lax.dot_general(
                    keys, query, (((1,), (1,)), ((), ())), preferred_element_type=jnp.float32
                )
                scores = jnp.where(keep, scores, MASKED)
                new_peak = jnp.maximum(peak, jnp.max(scores, axis=0, keepdims=True))
                weights = jnp.exp2((scores - new_peak) * EXP2_SCALE)
                shrink = jnp.exp2((peak - new_peak) * EXP2_SCALE)
                total = total * shrink + jnp.sum(weights, axis=0, keepdims=True)
                summed = summed * shrink + lax.dot_general(
                    values,
                    weights.astype(jnp.bfloat16),
                    (((0,), (0,)), ((), ())),
                    preferred_element_type=jnp.float32,
                )
                result.append((new_peak, total, summed))
            return tuple(result)

        state = tuple(
            (
                jnp.full((1, QUERY_BLOCK), MASKED, jnp.float32),
                jnp.zeros((1, QUERY_BLOCK), jnp.float32),
                jnp.zeros((HEAD, QUERY_BLOCK), jnp.float32),
            )
            for _ in heads
        )
        for part, pair_ref in enumerate((before_ref, own_ref, after_ref)):
            first_key = (0, SEG_MAX, SEG_MAX + row_count)[part]
            state = lax.fori_loop(
                bounds[block, 2 * part],
                bounds[block, 2 * part + 1],
                functools.partial(step, pair_ref, first_key),
                state,
            )
        for head, (peak, total, summed) in zip(heads, state):
            attended_ref[rows, head] = (summed * (1.0 / total)).T.astype(jnp.bfloat16)
    out_ref[...] = jnp.dot(
        place_ref[...], attended_ref[...], preferred_element_type=jnp.float32
    ).astype(jnp.bfloat16)


def attend_and_place(queries, first_column, before, own, after, query_seg, key_seg, bounds, placement):
    row_count = queries.shape[0]
    slot_count = placement.shape[0]
    width = before.shape[2]
    step_width = HEADS_PER_STEP * HEAD
    first_step = first_column // step_width
    whole = lambda shape: pl.BlockSpec(shape, lambda i, b: (0,) * len(shape))
    return pl.pallas_call(
        attend_kernel,
        out_shape=jax.ShapeDtypeStruct((slot_count, width), jnp.bfloat16),
        grid_spec=pltpu.PrefetchScalarGridSpec(
            num_scalar_prefetch=1,
            grid=(width // step_width,),
            in_specs=[
                pl.BlockSpec((row_count, step_width), lambda i, b: (0, first_step + i)),
                pl.BlockSpec((2, SEG_MAX, step_width), lambda i, b: (0, 0, i)),
                pl.BlockSpec((2, row_count, step_width), lambda i, b: (0, 0, first_step + i)),
                pl.BlockSpec((2, SEG_MAX, step_width), lambda i, b: (0, 0, i)),
                whole((1, row_count)),
                whole((row_count + 2 * SEG_MAX, 1)),
                whole((slot_count, row_count)),
            ],
            out_specs=pl.BlockSpec((slot_count, step_width), lambda i, b: (0, i)),
            scratch_shapes=[pltpu.VMEM((row_count, step_width), jnp.bfloat16)],
        ),
        compiler_params=pltpu.CompilerParams(vmem_limit_bytes=48 << 20),
        name="attend",
    )(bounds, queries, before, own, after, query_seg, key_seg, placement)


def key_ranges(segment_ids, query_seg, first_row):
    row_count = query_seg.shape[0]
    firsts = query_seg[::QUERY_BLOCK]
    lasts = query_seg[QUERY_BLOCK - 1 :: QUERY_BLOCK]
    low = jnp.sum((segment_ids[None, :] < firsts[:, None]).astype(jnp.int32), axis=1)
    high = jnp.sum((segment_ids[None, :] <= lasts[:, None]).astype(jnp.int32), axis=1)
    columns = []
    for start, length in ((-SEG_MAX, SEG_MAX), (0, row_count), (row_count, SEG_MAX)):
        part_low = jnp.clip(low - first_row - start, 0, length)
        part_high = jnp.clip(high - first_row - start, 0, length)
        columns += [part_low // KEY_BLOCK, (part_high + KEY_BLOCK - 1) // KEY_BLOCK]
    return jnp.stack(columns, axis=1)


def body(
    queries, keys_values, segment_ids, route_shard, route_slot, control_proj, base_hidden, cotangent
):
    row_count = queries.shape[0]
    width = queries.shape[1]
    model_width = control_proj.shape[1]
    shard_count = lax.axis_size("seq")
    shard_index = lax.axis_index("seq")
    capacity = 2 * row_count // shard_count
    slot_count = shard_count * capacity
    block_rows = width // shard_count
    far_count = shard_count // 4

    def swap(value, bit):
        return lax.ppermute(value, "seq", [(i, i ^ bit) for i in range(shard_count)])

    up = [(i, i + 1) for i in range(shard_count - 1)]
    down = [(j, i) for i, j in up]
    chunk_width = width // HEAD_CHUNKS
    halos = []
    for chunk in range(HEAD_CHUNKS):
        columns = slice(chunk * chunk_width, (chunk + 1) * chunk_width)
        before = lax.ppermute(keys_values[:, row_count - SEG_MAX :, columns], "seq", up)
        after = lax.ppermute(keys_values[:, :SEG_MAX, columns], "seq", down)
        halos.append((before, after))
    peer_cotangent = swap(cotangent, 1)

    target_shard = route_shard[:, 0]
    one_hot = (target_shard[:, None] == jnp.arange(shard_count, dtype=jnp.int32)[None, :]).astype(
        jnp.int32
    )
    slot_rank = jnp.sum((jnp.cumsum(one_hot, axis=0) - 1) * one_hot, axis=1)
    flat_place = target_shard * capacity + slot_rank
    place_mask = flat_place[None, :] == jnp.arange(slot_count, dtype=jnp.int32)[:, None]
    placement = place_mask.astype(jnp.bfloat16)
    occupied = jnp.sum(place_mask.astype(jnp.int32), axis=1)
    slot_values = jnp.sum(jnp.where(place_mask, route_slot[None, :], 0), axis=1)
    slot_table = jnp.where(occupied > 0, slot_values, -1).reshape(shard_count, capacity)
    incoming_slots = lax.all_to_all(slot_table, "seq", split_axis=0, concat_axis=0, tiled=True)
    landing = (
        incoming_slots.reshape(-1)[:, None] == jnp.arange(row_count, dtype=jnp.int32)[None, :]
    ).astype(jnp.bfloat16)

    first_row = shard_index * row_count
    query_seg = lax.dynamic_slice_in_dim(segment_ids, first_row, row_count)
    padded_seg = jnp.pad(segment_ids, (SEG_MAX, SEG_MAX), constant_values=-1)
    key_seg = lax.dynamic_slice_in_dim(padded_seg, first_row, row_count + 2 * SEG_MAX)
    bounds = key_ranges(segment_ids, query_seg, first_row)

    landed = []
    for chunk, (before, after) in enumerate(halos):
        outgoing = attend_and_place(
            queries, chunk * chunk_width, before, keys_values, after,
            query_seg[None, :], key_seg[:, None], bounds, placement,
        )
        incoming = lax.all_to_all(
            outgoing.reshape(shard_count, capacity, chunk_width),
            "seq",
            split_axis=0,
            concat_axis=0,
            tiled=True,
        )
        landed.append(
            jnp.einsum(
                "sk,sr->kr",
                incoming.reshape(slot_count, chunk_width),
                landing,
                preferred_element_type=jnp.float32,
            ).astype(jnp.bfloat16)
        )
    landed = jnp.concatenate(landed, axis=0)

    core = shard_index % 2
    near = (shard_index // 2) % 2
    far = shard_index // 4
    by_core = landed.reshape(2 * far_count, 2, block_rows, row_count)
    peer_landed = swap(lax.dynamic_index_in_dim(by_core, 1 - core, 1, keepdims=False), 1)
    own_landed = lax.dynamic_index_in_dim(by_core, core, 1, keepdims=False)
    both_landed = jnp.concatenate([own_landed, peer_landed], axis=2)
    by_near = both_landed.reshape(far_count, 2, block_rows, 2 * row_count)
    sent_rows = lax.dynamic_index_in_dim(by_near, 1 - near, 1, keepdims=False)
    kept_rows = lax.dynamic_index_in_dim(by_near, near, 1, keepdims=False)
    both_cotangent = jnp.concatenate([cotangent, peer_cotangent], axis=0)
    grad_pieces = []
    grad_width = model_width // GRAD_CHUNKS
    for chunk in range(GRAD_CHUNKS):
        columns = slice(chunk * grad_width, (chunk + 1) * grad_width)
        product = lambda rows: jnp.einsum(
            "fbt,td->fbd", rows, both_cotangent[:, columns], preferred_element_type=jnp.float32
        )
        arrived = swap(product(sent_rows).astype(jnp.bfloat16), 2)
        summed = product(kept_rows) + arrived.astype(jnp.float32)
        total = lax.dynamic_index_in_dim(summed, far, 0, keepdims=False)
        rounded = summed.astype(jnp.bfloat16)
        for other in range(1, far_count):
            piece = lax.dynamic_index_in_dim(rounded, far ^ other, 0, keepdims=False)
            total = total + swap(piece, 4 * other).astype(jnp.float32)
        grad_pieces.append(total)
    proj_grad = jnp.concatenate(grad_pieces, axis=1)

    added = jnp.einsum("kr,kd->rd", landed, control_proj, preferred_element_type=jnp.float32)
    mixed_hidden = (base_hidden.astype(jnp.float32) + added).astype(jnp.bfloat16)
    return (mixed_hidden, proj_grad)


def solution(mesh):
    placed = (
        P(("grp", "seq"), None),
        P(None, ("grp", "seq"), None),
        P("grp"),
        P(("grp", "seq"), None),
        P(("grp", "seq")),
        P(),
        P(("grp", "seq"), None),
        P(("grp", "seq"), None),
    )
    return jax.shard_map(
        body,
        mesh=mesh,
        in_specs=placed,
        out_specs=(P(("grp", "seq"), None), P(("grp", "seq"), None)),
        check_vma=False,
    )
```

```python
import functools
import math

import jax
import jax.numpy as jnp
from jax import lax
from jax.experimental import pallas as pl
from jax.experimental.pallas import tpu as pltpu
from jax.sharding import PartitionSpec as P

HEAD = 128
SEG_MAX = 512
LOCAL_QUERY_BLOCK = 256
HALO_QUERY_BLOCK = 128
KEY_BLOCK = 256
HEADS_PER_STEP = 3
STEP_WIDTH = HEADS_PER_STEP * HEAD
OUTER_PARTS = 2
INNER_PARTS = 2
LOCAL_FLOPS_HINT = 1 << 33
HALO_FLOPS_HINT = 1 << 34
MASKED = -1e30
EXP2_SCALE = HEAD ** (-0.5) * math.log2(math.e)
HEAD_SLICES = [slice(h * HEAD, (h + 1) * HEAD) for h in range(HEADS_PER_STEP)]


def attend_step(pair_ref, key_seg_ref, query_seg, queries, key_block, state):
    offset = pl.multiple_of(key_block * KEY_BLOCK, KEY_BLOCK)
    keep = key_seg_ref[pl.ds(offset, KEY_BLOCK), :] == query_seg
    result = []
    for head, query, (peak, total, summed) in zip(HEAD_SLICES, queries, state):
        keys = pair_ref[0, pl.ds(offset, KEY_BLOCK), head]
        values = pair_ref[1, pl.ds(offset, KEY_BLOCK), head]
        scores = lax.dot_general(
            keys, query, (((1,), (1,)), ((), ())), preferred_element_type=jnp.float32
        )
        scores = jnp.where(keep, scores, MASKED)
        new_peak = jnp.maximum(peak, jnp.max(scores, axis=0, keepdims=True))
        weights = jnp.exp2((scores - new_peak) * EXP2_SCALE)
        shrink = jnp.exp2((peak - new_peak) * EXP2_SCALE)
        total = total * shrink + jnp.sum(weights, axis=0, keepdims=True)
        summed = summed * shrink + lax.dot_general(
            values,
            weights.astype(jnp.bfloat16),
            (((0,), (0,)), ((), ())),
            preferred_element_type=jnp.float32,
        )
        result.append((new_peak, total, summed))
    return tuple(result)


def local_kernel(bounds, query_ref, own_ref, query_seg_ref, key_seg_ref, summed_ref, stats_ref):
    row_count = query_ref.shape[0]
    for block in range(row_count // LOCAL_QUERY_BLOCK):
        rows = slice(block * LOCAL_QUERY_BLOCK, (block + 1) * LOCAL_QUERY_BLOCK)
        state = tuple(
            (
                jnp.full((1, LOCAL_QUERY_BLOCK), MASKED, jnp.float32),
                jnp.zeros((1, LOCAL_QUERY_BLOCK), jnp.float32),
                jnp.zeros((HEAD, LOCAL_QUERY_BLOCK), jnp.float32),
            )
            for _ in HEAD_SLICES
        )
        state = lax.fori_loop(
            bounds[block, 2],
            bounds[block, 3],
            functools.partial(
                attend_step,
                own_ref,
                key_seg_ref,
                query_seg_ref[:, rows],
                [query_ref[rows, head] for head in HEAD_SLICES],
            ),
            state,
        )
        for h, (peak, total, summed) in enumerate(state):
            stats_ref[0, h : h + 1, rows] = peak
            stats_ref[0, HEADS_PER_STEP + h : HEADS_PER_STEP + h + 1, rows] = total
            summed_ref[HEAD_SLICES[h], rows] = summed


def halo_kernel(
    bounds, query_ref, before_ref, after_ref, query_seg_ref, before_seg_ref, after_seg_ref,
    summed_ref, stats_ref, place_ref, out_ref, attended_ref,
):
    row_count = query_ref.shape[0]
    for block in range(row_count // HALO_QUERY_BLOCK):
        rows = slice(block * HALO_QUERY_BLOCK, (block + 1) * HALO_QUERY_BLOCK)
        queries = [query_ref[rows, head] for head in HEAD_SLICES]
        query_seg = query_seg_ref[:, rows]
        state = tuple(
            (
                stats_ref[0, h : h + 1, rows],
                stats_ref[0, HEADS_PER_STEP + h : HEADS_PER_STEP + h + 1, rows],
                summed_ref[head, rows],
            )
            for h, head in enumerate(HEAD_SLICES)
        )
        for column, pair_ref, seg_ref in ((0, before_ref, before_seg_ref), (4, after_ref, after_seg_ref)):
            state = lax.fori_loop(
                bounds[block, column],
                bounds[block, column + 1],
                functools.partial(attend_step, pair_ref, seg_ref, query_seg, queries),
                state,
            )
        for head, (peak, total, summed) in zip(HEAD_SLICES, state):
            attended_ref[rows, head] = (summed * (1.0 / total)).T.astype(jnp.bfloat16)
    out_ref[...] = jnp.dot(
        place_ref[...], attended_ref[...], preferred_element_type=jnp.float32
    ).astype(jnp.bfloat16)


def whole(*shape):
    return pl.BlockSpec(shape, lambda i, b: (0,) * len(shape))


def step_column(steps):
    return lambda i, b: (0, steps[0] + steps[1] * i)


def step_pair(steps):
    return lambda i, b: (0, 0, steps[0] + steps[1] * i)


def attend_local(queries, pairs, steps, query_seg, bounds):
    row_count = queries.shape[0]
    width = 2 * STEP_WIDTH
    return pl.pallas_call(
        local_kernel,
        out_shape=(
            jax.ShapeDtypeStruct((width, row_count), jnp.float32),
            jax.ShapeDtypeStruct((2, 2 * HEADS_PER_STEP, row_count), jnp.float32),
        ),
        grid_spec=pltpu.PrefetchScalarGridSpec(
            num_scalar_prefetch=1,
            grid=(2,),
            in_specs=[
                pl.BlockSpec((row_count, STEP_WIDTH), step_column(steps)),
                pl.BlockSpec((2, row_count, STEP_WIDTH), step_pair(steps)),
                whole(1, row_count),
                whole(row_count, 1),
            ],
            out_specs=[
                pl.BlockSpec((STEP_WIDTH, row_count), lambda i, b: (i, 0)),
                pl.BlockSpec((1, 2 * HEADS_PER_STEP, row_count), lambda i, b: (i, 0, 0)),
            ],
        ),
        compiler_params=pltpu.CompilerParams(vmem_limit_bytes=48 << 20),
        cost_estimate=pl.CostEstimate(
            flops=LOCAL_FLOPS_HINT, transcendentals=1 << 20, bytes_accessed=1 << 22
        ),
        name="attend_local",
    )(bounds, queries, pairs, query_seg[None, :], query_seg[:, None])


def attend_halo(queries, halo, steps, query_seg, margin_seg, bounds, local, placement):
    row_count = queries.shape[0]
    slot_count = placement.shape[0]
    before, after = halo
    return pl.pallas_call(
        halo_kernel,
        out_shape=jax.ShapeDtypeStruct((slot_count, 2 * STEP_WIDTH), jnp.bfloat16),
        grid_spec=pltpu.PrefetchScalarGridSpec(
            num_scalar_prefetch=1,
            grid=(2,),
            in_specs=[
                pl.BlockSpec((row_count, STEP_WIDTH), step_column(steps)),
                pl.BlockSpec((2, SEG_MAX, STEP_WIDTH), step_pair((0, 1))),
                pl.BlockSpec((2, SEG_MAX, STEP_WIDTH), step_pair((0, 1))),
                whole(1, row_count),
                whole(SEG_MAX, 1),
                whole(SEG_MAX, 1),
                pl.BlockSpec((STEP_WIDTH, row_count), lambda i, b: (i, 0)),
                pl.BlockSpec((1, 2 * HEADS_PER_STEP, row_count), lambda i, b: (i, 0, 0)),
                whole(slot_count, row_count),
            ],
            out_specs=pl.BlockSpec((slot_count, STEP_WIDTH), step_column((0, 1))),
            scratch_shapes=[pltpu.VMEM((row_count, STEP_WIDTH), jnp.bfloat16)],
        ),
        compiler_params=pltpu.CompilerParams(vmem_limit_bytes=48 << 20),
        cost_estimate=pl.CostEstimate(
            flops=HALO_FLOPS_HINT, transcendentals=1 << 20, bytes_accessed=1 << 22
        ),
        name="attend_halo",
    )(
        bounds, queries, before, after, query_seg[None, :],
        margin_seg[:SEG_MAX, None], margin_seg[SEG_MAX + row_count :, None], *local, placement,
    )


def key_ranges(segment_ids, query_seg, first_row, query_block):
    row_count = query_seg.shape[0]
    firsts = query_seg[::query_block]
    lasts = query_seg[query_block - 1 :: query_block]
    low = jnp.sum((segment_ids[None, :] < firsts[:, None]).astype(jnp.int32), axis=1)
    high = jnp.sum((segment_ids[None, :] <= lasts[:, None]).astype(jnp.int32), axis=1)
    columns = []
    for start, length in ((-SEG_MAX, SEG_MAX), (0, row_count), (row_count, SEG_MAX)):
        part_low = jnp.clip(low - first_row - start, 0, length)
        part_high = jnp.clip(high - first_row - start, 0, length)
        columns += [part_low // KEY_BLOCK, (part_high + KEY_BLOCK - 1) // KEY_BLOCK]
    return jnp.stack(columns, axis=1)


def body(
    queries, keys_values, segment_ids, route_shard, route_slot, control_proj, base_hidden, cotangent
):
    row_count = queries.shape[0]
    width = queries.shape[1]
    model_width = control_proj.shape[1]
    shard_count = lax.axis_size("seq")
    shard_index = lax.axis_index("seq")
    capacity = 2 * row_count // shard_count
    slot_count = shard_count * capacity
    block_rows = width // shard_count
    far_count = shard_count // 4
    core = shard_index % 2
    near = (shard_index // 2) % 2
    far = shard_index // 4
    quarter = width // 4
    far_quarter = far_count // 4

    def swap(value, bit):
        return lax.ppermute(value, "seq", [(i, i ^ bit) for i in range(shard_count)])

    def outer(value):
        return jnp.concatenate([value[..., :quarter], value[..., 3 * quarter :]], axis=-1)

    def inner(value):
        return value[..., quarter : 3 * quarter]

    up = [(i, i + 1) for i in range(shard_count - 1)]
    down = [(j, i) for i, j in up]

    def halo(pairs):
        before = lax.ppermute(pairs[:, row_count - SEG_MAX :], "seq", up)
        after = lax.ppermute(pairs[:, :SEG_MAX], "seq", down)
        return before, after

    first_halo = halo(outer(keys_values))
    gated, first_halo = lax.optimization_barrier((inner(keys_values), first_halo))
    second_halo = halo(gated)
    peer_cotangent = swap(cotangent, 1)

    target_shard = route_shard[:, 0]
    one_hot = (target_shard[:, None] == jnp.arange(shard_count, dtype=jnp.int32)[None, :]).astype(
        jnp.int32
    )
    slot_rank = jnp.sum((jnp.cumsum(one_hot, axis=0) - 1) * one_hot, axis=1)
    flat_place = target_shard * capacity + slot_rank
    place_mask = flat_place[None, :] == jnp.arange(slot_count, dtype=jnp.int32)[:, None]
    placement = place_mask.astype(jnp.bfloat16)
    occupied = jnp.sum(place_mask.astype(jnp.int32), axis=1)
    slot_values = jnp.sum(jnp.where(place_mask, route_slot[None, :], 0), axis=1)
    slot_table = jnp.where(occupied > 0, slot_values, -1).reshape(shard_count, capacity)
    incoming_slots = lax.all_to_all(slot_table, "seq", split_axis=0, concat_axis=0, tiled=True)
    landing = (
        incoming_slots.reshape(-1)[:, None] == jnp.arange(row_count, dtype=jnp.int32)[None, :]
    ).astype(jnp.bfloat16)

    first_row = shard_index * row_count
    query_seg = lax.dynamic_slice_in_dim(segment_ids, first_row, row_count)
    padded_seg = jnp.pad(segment_ids, (SEG_MAX, SEG_MAX), constant_values=-1)
    key_seg = lax.dynamic_slice_in_dim(padded_seg, first_row, row_count + 2 * SEG_MAX)
    local_bounds = key_ranges(segment_ids, query_seg, first_row, LOCAL_QUERY_BLOCK)
    halo_bounds = key_ranges(segment_ids, query_seg, first_row, HALO_QUERY_BLOCK)
    head_steps = ((0, 3), (1, 1))
    outer_local = attend_local(queries, keys_values, head_steps[0], query_seg, local_bounds)
    inner_local = attend_local(queries, keys_values, head_steps[1], query_seg, local_bounds)
    outer_local, inner_local, first_halo = lax.optimization_barrier(
        (outer_local, inner_local, first_halo)
    )
    outer_placed = attend_halo(
        queries, first_halo, head_steps[0], query_seg, key_seg, halo_bounds, outer_local, placement
    )
    inner_placed = attend_halo(
        queries, second_halo, head_steps[1], query_seg, key_seg, halo_bounds, inner_local, placement
    )

    def split_columns(parts):
        step = model_width // parts
        return [slice(part * step, (part + 1) * step) for part in range(parts)]

    def product(halves, columns):
        return sum(
            jnp.einsum("fbt,td->fbd", half, other[:, columns], preferred_element_type=jnp.float32)
            for half, other in zip(halves, (cotangent, peer_cotangent))
        )

    def land(value):
        incoming = lax.all_to_all(
            value.reshape(shard_count, capacity, 2 * quarter),
            "seq",
            split_axis=0,
            concat_axis=0,
            tiled=True,
        )
        return jnp.einsum(
            "sk,sr->kr",
            incoming.reshape(slot_count, 2 * quarter),
            landing,
            preferred_element_type=jnp.float32,
        ).astype(jnp.bfloat16)

    def near_reduce(rows, parts):
        by_core = rows.reshape(far_count, 2, block_rows, row_count)
        peer_rows = swap(lax.dynamic_index_in_dim(by_core, 1 - core, 1, keepdims=False), 1)
        own_rows = lax.dynamic_index_in_dim(by_core, core, 1, keepdims=False)
        by_near = [
            value.reshape(far_count // 2, 2, block_rows, row_count) for value in (own_rows, peer_rows)
        ]
        sent_rows = [lax.dynamic_index_in_dim(v, 1 - near, 1, keepdims=False) for v in by_near]
        kept_rows = [lax.dynamic_index_in_dim(v, near, 1, keepdims=False) for v in by_near]
        sent = [product(sent_rows, columns).astype(jnp.bfloat16) for columns in split_columns(parts)]
        summed = [
            product(kept_rows, columns) + swap(value, 2).astype(jnp.float32)
            for columns, value in zip(split_columns(parts), sent)
        ]
        return sent, summed

    def far_exchange(chunk, summed):
        members = [
            f for f in range(far_count) if (far_quarter <= f < 3 * far_quarter) == (chunk == 1)
        ]

        def place_of(index):
            if chunk == 1:
                return index - far_quarter
            return jnp.where(index < far_quarter, index, index - 2 * far_quarter)

        kept = lax.dynamic_index_in_dim(summed, place_of(far), 0, keepdims=False)
        rounded = summed.astype(jnp.bfloat16)
        arrived = []
        for other in range(1, far_count):
            piece = lax.dynamic_index_in_dim(rounded, place_of(far ^ other), 0, keepdims=False)
            routes = [
                (i, i ^ (4 * other)) for i in range(shard_count) if (i // 4) ^ other in members
            ]
            arrived.append(lax.ppermute(piece, "seq", routes))
        return kept, arrived

    def far_total(kept, arrived):
        return kept + sum(value.astype(jnp.float32) for value in arrived)

    outer_rows = land(outer_placed)
    _, outer_summed = near_reduce(outer_rows, OUTER_PARTS)
    outer_far = [far_exchange(0, value) for value in outer_summed]
    inner_rows = land(inner_placed)
    _, inner_summed = near_reduce(inner_rows, INNER_PARTS)
    outer_far, late_rows, inner_summed[0] = lax.optimization_barrier(
        (outer_far, inner_rows, inner_summed[0])
    )
    inner_far = [far_exchange(1, value) for value in inner_summed]
    grad_parts = [
        jnp.concatenate([far_total(*pair) for pair in pairs], axis=1)
        for pairs in (outer_far, inner_far)
    ]
    in_middle = (far >= far_quarter) & (far < 3 * far_quarter)
    proj_grad = jnp.where(in_middle, grad_parts[1], grad_parts[0])

    added = jnp.einsum(
        "kr,kd->rd",
        jnp.concatenate([outer_rows[:quarter], late_rows, outer_rows[quarter:]], axis=0),
        control_proj,
        preferred_element_type=jnp.float32,
    )
    mixed_hidden = (base_hidden.astype(jnp.float32) + added).astype(jnp.bfloat16)
    return (mixed_hidden, proj_grad)


def solution(mesh):
    placed = (
        P(("grp", "seq"), None),
        P(None, ("grp", "seq"), None),
        P("grp"),
        P(("grp", "seq"), None),
        P(("grp", "seq")),
        P(),
        P(("grp", "seq"), None),
        P(("grp", "seq"), None),
    )
    return jax.shard_map(
        body,
        mesh=mesh,
        in_specs=placed,
        out_specs=(P(("grp", "seq"), None), P(("grp", "seq"), None)),
        check_vma=False,
    )
```

```python
import functools
import math

import jax
import jax.numpy as jnp
from jax import lax
from jax.experimental import pallas as pl
from jax.experimental.pallas import tpu as pltpu
from jax.sharding import PartitionSpec as P

HEAD = 128
SEG_MAX = 512
QUERY_BLOCK = 128
KEY_BLOCK = 256
OUTER_PARTS = 2
INNER_PARTS = 2
LOCAL_FLOPS_HINT = 1 << 33
HALO_FLOPS_HINT = 1 << 34
MASKED = -1e30
EXP2_SCALE = HEAD ** (-0.5) * math.log2(math.e)


def attend_step(pairs, key_seg_ref, query_seg, queries, key_block, state):
    offset = pl.multiple_of(key_block * KEY_BLOCK, KEY_BLOCK)
    keep = key_seg_ref[pl.ds(offset, KEY_BLOCK), :] == query_seg
    result = []
    for (pair_ref, head), query, (peak, total, summed) in zip(pairs, queries, state):
        keys = pair_ref[0, pl.ds(offset, KEY_BLOCK), head]
        values = pair_ref[1, pl.ds(offset, KEY_BLOCK), head]
        scores = lax.dot_general(
            keys, query, (((1,), (1,)), ((), ())), preferred_element_type=jnp.float32
        )
        scores = jnp.where(keep, scores, MASKED)
        new_peak = jnp.maximum(peak, jnp.max(scores, axis=0, keepdims=True))
        weights = jnp.exp2((scores - new_peak) * EXP2_SCALE)
        shrink = jnp.exp2((peak - new_peak) * EXP2_SCALE)
        total = total * shrink + jnp.sum(weights, axis=0, keepdims=True)
        summed = summed * shrink + lax.dot_general(
            values,
            weights.astype(jnp.bfloat16),
            (((0,), (0,)), ((), ())),
            preferred_element_type=jnp.float32,
        )
        result.append((new_peak, total, summed))
    return tuple(result)


def head_slices(width):
    return [slice(start, start + HEAD) for start in range(0, width, HEAD)]


def local_kernel(
    bounds, first_query_ref, last_query_ref, first_own_ref, last_own_ref, query_seg_ref,
    key_seg_ref, summed_ref, stats_ref,
):
    row_count, width = first_query_ref.shape
    heads = head_slices(width)
    for block in range(row_count // QUERY_BLOCK):
        rows = slice(block * QUERY_BLOCK, (block + 1) * QUERY_BLOCK)
        state = tuple(
            (
                jnp.full((1, QUERY_BLOCK), MASKED, jnp.float32),
                jnp.zeros((1, QUERY_BLOCK), jnp.float32),
                jnp.zeros((HEAD, QUERY_BLOCK), jnp.float32),
            )
            for _ in range(2 * len(heads))
        )
        state = lax.fori_loop(
            bounds[block, 2],
            bounds[block, 3],
            functools.partial(
                attend_step,
                [(ref, head) for ref in (first_own_ref, last_own_ref) for head in heads],
                key_seg_ref,
                query_seg_ref[:, rows],
                [ref[rows, head] for ref in (first_query_ref, last_query_ref) for head in heads],
            ),
            state,
        )
        for h, (peak, total, summed) in enumerate(state):
            stats_ref[0, h : h + 1, rows] = peak
            stats_ref[1, h : h + 1, rows] = total
            summed_ref[h * HEAD : (h + 1) * HEAD, rows] = summed


def halo_kernel(
    bounds, first_query_ref, last_query_ref, before_ref, after_ref, query_seg_ref,
    before_seg_ref, after_seg_ref, summed_ref, stats_ref, place_ref, out_ref, attended_ref,
):
    row_count, half_width = first_query_ref.shape
    heads = head_slices(2 * half_width)
    for block in range(row_count // QUERY_BLOCK):
        rows = slice(block * QUERY_BLOCK, (block + 1) * QUERY_BLOCK)
        queries = [
            ref[rows, head]
            for ref in (first_query_ref, last_query_ref)
            for head in head_slices(half_width)
        ]
        query_seg = query_seg_ref[:, rows]
        state = tuple(
            (stats_ref[0, h : h + 1, rows], stats_ref[1, h : h + 1, rows], summed_ref[head, rows])
            for h, head in enumerate(heads)
        )
        for column, pair_ref, seg_ref in ((0, before_ref, before_seg_ref), (4, after_ref, after_seg_ref)):
            state = lax.fori_loop(
                bounds[block, column],
                bounds[block, column + 1],
                functools.partial(
                    attend_step, [(pair_ref, head) for head in heads], seg_ref, query_seg, queries
                ),
                state,
            )
        for head, (peak, total, summed) in zip(heads, state):
            attended_ref[rows, head] = (summed * (1.0 / total)).T.astype(jnp.bfloat16)
    out_ref[...] = jnp.dot(
        place_ref[...], attended_ref[...], preferred_element_type=jnp.float32
    ).astype(jnp.bfloat16)


def whole(*shape):
    return pl.BlockSpec(shape, lambda i, b: (0,) * len(shape))


def at_column(shape, column):
    return pl.BlockSpec(shape, lambda i, b: (0,) * (len(shape) - 1) + (column,))


def attend_local(queries, pairs, quarters, query_seg, bounds):
    row_count, width = queries.shape
    quarter = width // 4
    head_count = width // (2 * HEAD)
    return pl.pallas_call(
        local_kernel,
        out_shape=(
            jax.ShapeDtypeStruct((2 * quarter, row_count), jnp.float32),
            jax.ShapeDtypeStruct((2, head_count, row_count), jnp.float32),
        ),
        grid_spec=pltpu.PrefetchScalarGridSpec(
            num_scalar_prefetch=1,
            grid=(1,),
            in_specs=[at_column((row_count, quarter), q) for q in quarters]
            + [at_column((2, row_count, quarter), q) for q in quarters]
            + [whole(1, row_count), whole(row_count, 1)],
            out_specs=[whole(2 * quarter, row_count), whole(2, head_count, row_count)],
        ),
        compiler_params=pltpu.CompilerParams(vmem_limit_bytes=48 << 20),
        cost_estimate=pl.CostEstimate(
            flops=LOCAL_FLOPS_HINT, transcendentals=1 << 20, bytes_accessed=1 << 22
        ),
        name="attend_local",
    )(bounds, queries, queries, pairs, pairs, query_seg[None, :], query_seg[:, None])


def attend_halo(queries, halo, quarters, query_seg, margin_seg, bounds, local, placement):
    row_count, width = queries.shape
    quarter = width // 4
    head_count = width // (2 * HEAD)
    slot_count = placement.shape[0]
    return pl.pallas_call(
        halo_kernel,
        out_shape=jax.ShapeDtypeStruct((slot_count, 2 * quarter), jnp.bfloat16),
        grid_spec=pltpu.PrefetchScalarGridSpec(
            num_scalar_prefetch=1,
            grid=(1,),
            in_specs=[at_column((row_count, quarter), q) for q in quarters]
            + [whole(2, SEG_MAX, 2 * quarter)] * 2
            + [
                whole(1, row_count),
                whole(SEG_MAX, 1),
                whole(SEG_MAX, 1),
                whole(2 * quarter, row_count),
                whole(2, head_count, row_count),
                whole(slot_count, row_count),
            ],
            out_specs=whole(slot_count, 2 * quarter),
            scratch_shapes=[pltpu.VMEM((row_count, 2 * quarter), jnp.bfloat16)],
        ),
        compiler_params=pltpu.CompilerParams(vmem_limit_bytes=48 << 20),
        cost_estimate=pl.CostEstimate(
            flops=HALO_FLOPS_HINT, transcendentals=1 << 20, bytes_accessed=1 << 22
        ),
        name="attend_halo",
    )(
        bounds, queries, queries, *halo, query_seg[None, :], margin_seg[:SEG_MAX, None],
        margin_seg[SEG_MAX + row_count :, None], *local, placement,
    )


def key_ranges(segment_ids, query_seg, first_row):
    row_count = query_seg.shape[0]
    firsts = query_seg[::QUERY_BLOCK]
    lasts = query_seg[QUERY_BLOCK - 1 :: QUERY_BLOCK]
    low = jnp.sum((segment_ids[None, :] < firsts[:, None]).astype(jnp.int32), axis=1)
    high = jnp.sum((segment_ids[None, :] <= lasts[:, None]).astype(jnp.int32), axis=1)
    columns = []
    for start, length in ((-SEG_MAX, SEG_MAX), (0, row_count), (row_count, SEG_MAX)):
        part_low = jnp.clip(low - first_row - start, 0, length)
        part_high = jnp.clip(high - first_row - start, 0, length)
        columns += [part_low // KEY_BLOCK, (part_high + KEY_BLOCK - 1) // KEY_BLOCK]
    return jnp.stack(columns, axis=1)


def body(
    queries, keys_values, segment_ids, route_shard, route_slot, control_proj, base_hidden, cotangent
):
    row_count = queries.shape[0]
    width = queries.shape[1]
    model_width = control_proj.shape[1]
    shard_count = lax.axis_size("seq")
    shard_index = lax.axis_index("seq")
    capacity = 2 * row_count // shard_count
    slot_count = shard_count * capacity
    block_rows = width // shard_count
    far_count = shard_count // 4
    core = shard_index % 2
    near = (shard_index // 2) % 2
    far = shard_index // 4
    quarter = width // 4
    far_quarter = far_count // 4

    def swap(value, bit):
        return lax.ppermute(value, "seq", [(i, i ^ bit) for i in range(shard_count)])

    def outer(value):
        return jnp.concatenate([value[..., :quarter], value[..., 3 * quarter :]], axis=-1)

    def inner(value):
        return value[..., quarter : 3 * quarter]

    up = [(i, i + 1) for i in range(shard_count - 1)]
    down = [(j, i) for i, j in up]

    def halo(pairs):
        before = lax.ppermute(pairs[:, row_count - SEG_MAX :], "seq", up)
        after = lax.ppermute(pairs[:, :SEG_MAX], "seq", down)
        return before, after

    first_halo = halo(outer(keys_values))
    gated, first_halo = lax.optimization_barrier((inner(keys_values), first_halo))
    second_halo = halo(gated)
    peer_cotangent = swap(cotangent, 1)

    target_shard = route_shard[:, 0]
    one_hot = (target_shard[:, None] == jnp.arange(shard_count, dtype=jnp.int32)[None, :]).astype(
        jnp.int32
    )
    slot_rank = jnp.sum((jnp.cumsum(one_hot, axis=0) - 1) * one_hot, axis=1)
    flat_place = target_shard * capacity + slot_rank
    place_mask = flat_place[None, :] == jnp.arange(slot_count, dtype=jnp.int32)[:, None]
    placement = place_mask.astype(jnp.bfloat16)
    occupied = jnp.sum(place_mask.astype(jnp.int32), axis=1)
    slot_values = jnp.sum(jnp.where(place_mask, route_slot[None, :], 0), axis=1)
    slot_table = jnp.where(occupied > 0, slot_values, -1).reshape(shard_count, capacity)
    incoming_slots = lax.all_to_all(slot_table, "seq", split_axis=0, concat_axis=0, tiled=True)
    landing = (
        incoming_slots.reshape(-1)[:, None] == jnp.arange(row_count, dtype=jnp.int32)[None, :]
    ).astype(jnp.bfloat16)

    first_row = shard_index * row_count
    query_seg = lax.dynamic_slice_in_dim(segment_ids, first_row, row_count)
    padded_seg = jnp.pad(segment_ids, (SEG_MAX, SEG_MAX), constant_values=-1)
    key_seg = lax.dynamic_slice_in_dim(padded_seg, first_row, row_count + 2 * SEG_MAX)
    bounds = key_ranges(segment_ids, query_seg, first_row)
    quarters = ((0, 3), (1, 2))
    outer_local = attend_local(queries, keys_values, quarters[0], query_seg, bounds)
    inner_local = attend_local(queries, keys_values, quarters[1], query_seg, bounds)
    outer_local, inner_local, first_halo = lax.optimization_barrier(
        (outer_local, inner_local, first_halo)
    )
    outer_placed = attend_halo(
        queries, first_halo, quarters[0], query_seg, key_seg, bounds, outer_local, placement
    )
    inner_placed = attend_halo(
        queries, second_halo, quarters[1], query_seg, key_seg, bounds, inner_local, placement
    )

    def split_columns(parts):
        step = model_width // parts
        return [slice(part * step, (part + 1) * step) for part in range(parts)]

    def product(halves, columns):
        return sum(
            jnp.einsum("fbt,td->fbd", half, other[:, columns], preferred_element_type=jnp.float32)
            for half, other in zip(halves, (cotangent, peer_cotangent))
        )

    def land(value):
        incoming = lax.all_to_all(
            value.reshape(shard_count, capacity, 2 * quarter),
            "seq",
            split_axis=0,
            concat_axis=0,
            tiled=True,
        )
        return jnp.einsum(
            "sk,sr->kr",
            incoming.reshape(slot_count, 2 * quarter),
            landing,
            preferred_element_type=jnp.float32,
        ).astype(jnp.bfloat16)

    def near_reduce(rows, parts):
        by_core = rows.reshape(far_count, 2, block_rows, row_count)
        peer_rows = swap(lax.dynamic_index_in_dim(by_core, 1 - core, 1, keepdims=False), 1)
        own_rows = lax.dynamic_index_in_dim(by_core, core, 1, keepdims=False)
        by_near = [
            value.reshape(far_count // 2, 2, block_rows, row_count) for value in (own_rows, peer_rows)
        ]
        sent_rows = [lax.dynamic_index_in_dim(v, 1 - near, 1, keepdims=False) for v in by_near]
        kept_rows = [lax.dynamic_index_in_dim(v, near, 1, keepdims=False) for v in by_near]
        sent = [product(sent_rows, columns).astype(jnp.bfloat16) for columns in split_columns(parts)]
        summed = [
            product(kept_rows, columns) + swap(value, 2).astype(jnp.float32)
            for columns, value in zip(split_columns(parts), sent)
        ]
        return sent, summed

    def far_exchange(chunk, summed):
        members = [
            f for f in range(far_count) if (far_quarter <= f < 3 * far_quarter) == (chunk == 1)
        ]

        def place_of(index):
            if chunk == 1:
                return index - far_quarter
            return jnp.where(index < far_quarter, index, index - 2 * far_quarter)

        kept = lax.dynamic_index_in_dim(summed, place_of(far), 0, keepdims=False)
        rounded = summed.astype(jnp.bfloat16)
        arrived = []
        for other in range(1, far_count):
            piece = lax.dynamic_index_in_dim(rounded, place_of(far ^ other), 0, keepdims=False)
            routes = [
                (i, i ^ (4 * other)) for i in range(shard_count) if (i // 4) ^ other in members
            ]
            arrived.append(lax.ppermute(piece, "seq", routes))
        return kept, arrived

    def far_total(kept, arrived):
        return kept + sum(value.astype(jnp.float32) for value in arrived)

    outer_rows = land(outer_placed)
    _, outer_summed = near_reduce(outer_rows, OUTER_PARTS)
    outer_far = [far_exchange(0, value) for value in outer_summed]
    inner_rows = land(inner_placed)
    _, inner_summed = near_reduce(inner_rows, INNER_PARTS)
    outer_far, late_rows, inner_summed[0] = lax.optimization_barrier(
        (outer_far, inner_rows, inner_summed[0])
    )
    inner_far = [far_exchange(1, value) for value in inner_summed]
    grad_parts = [
        jnp.concatenate([far_total(*pair) for pair in pairs], axis=1)
        for pairs in (outer_far, inner_far)
    ]
    in_middle = (far >= far_quarter) & (far < 3 * far_quarter)
    proj_grad = jnp.where(in_middle, grad_parts[1], grad_parts[0])

    added = jnp.einsum(
        "kr,kd->rd",
        jnp.concatenate([outer_rows[:quarter], late_rows, outer_rows[quarter:]], axis=0),
        control_proj,
        preferred_element_type=jnp.float32,
    )
    mixed_hidden = (base_hidden.astype(jnp.float32) + added).astype(jnp.bfloat16)
    return (mixed_hidden, proj_grad)


def solution(mesh):
    placed = (
        P(("grp", "seq"), None),
        P(None, ("grp", "seq"), None),
        P("grp"),
        P(("grp", "seq"), None),
        P(("grp", "seq")),
        P(),
        P(("grp", "seq"), None),
        P(("grp", "seq"), None),
    )
    return jax.shard_map(
        body,
        mesh=mesh,
        in_specs=placed,
        out_specs=(P(("grp", "seq"), None), P(("grp", "seq"), None)),
        check_vma=False,
    )
```

```python
import functools
import math

import jax
import jax.numpy as jnp
from jax import lax
from jax.experimental import pallas as pl
from jax.experimental.pallas import tpu as pltpu
from jax.sharding import PartitionSpec as P

HEAD = 128
SEG_MAX = 512
QUERY_BLOCK = 128
KEY_BLOCK = 256
OUTER_PARTS = 2
INNER_PARTS = 2
LOCAL_FLOPS_HINT = 1 << 33
HALO_FLOPS_HINT = 1 << 34
MASKED = -1e30
EXP2_SCALE = HEAD ** (-0.5) * math.log2(math.e)


def attend_step(pairs, key_seg_ref, query_seg, queries, key_block, state):
    offset = pl.multiple_of(key_block * KEY_BLOCK, KEY_BLOCK)
    keep = key_seg_ref[pl.ds(offset, KEY_BLOCK), :] == query_seg
    result = []
    for (pair_ref, head), query, (peak, total, summed) in zip(pairs, queries, state):
        keys = pair_ref[0, pl.ds(offset, KEY_BLOCK), head]
        values = pair_ref[1, pl.ds(offset, KEY_BLOCK), head]
        scores = lax.dot_general(
            keys, query, (((1,), (1,)), ((), ())), preferred_element_type=jnp.float32
        )
        scores = jnp.where(keep, scores, MASKED)
        new_peak = jnp.maximum(peak, jnp.max(scores, axis=0, keepdims=True))
        weights = jnp.exp2((scores - new_peak) * EXP2_SCALE)
        shrink = jnp.exp2((peak - new_peak) * EXP2_SCALE)
        total = total * shrink + jnp.sum(weights, axis=0, keepdims=True)
        summed = summed * shrink + lax.dot_general(
            values,
            weights.astype(jnp.bfloat16),
            (((0,), (0,)), ((), ())),
            preferred_element_type=jnp.float32,
        )
        result.append((new_peak, total, summed))
    return tuple(result)


def head_slices(width):
    return [slice(start, start + HEAD) for start in range(0, width, HEAD)]


def local_kernel(
    bounds, first_query_ref, last_query_ref, first_own_ref, last_own_ref, query_seg_ref,
    key_seg_ref, summed_ref, stats_ref,
):
    block = pl.program_id(0)
    heads = head_slices(first_query_ref.shape[1])
    state = tuple(
        (
            jnp.full((1, QUERY_BLOCK), MASKED, jnp.float32),
            jnp.zeros((1, QUERY_BLOCK), jnp.float32),
            jnp.zeros((HEAD, QUERY_BLOCK), jnp.float32),
        )
        for _ in range(2 * len(heads))
    )
    state = lax.fori_loop(
        bounds[block, 2],
        bounds[block, 3],
        functools.partial(
            attend_step,
            [(ref, head) for ref in (first_own_ref, last_own_ref) for head in heads],
            key_seg_ref,
            query_seg_ref[...],
            [ref[:, head] for ref in (first_query_ref, last_query_ref) for head in heads],
        ),
        state,
    )
    for h, (peak, total, summed) in enumerate(state):
        stats_ref[0, h : h + 1, :] = peak
        stats_ref[1, h : h + 1, :] = total
        summed_ref[h * HEAD : (h + 1) * HEAD, :] = summed


def halo_kernel(
    bounds, first_query_ref, last_query_ref, before_ref, after_ref, query_seg_ref,
    before_seg_ref, after_seg_ref, summed_ref, stats_ref, place_ref, out_ref, attended_ref,
):
    block = pl.program_id(0)
    half_width = first_query_ref.shape[1]
    heads = head_slices(2 * half_width)
    queries = [
        ref[:, head] for ref in (first_query_ref, last_query_ref) for head in head_slices(half_width)
    ]
    state = tuple(
        (stats_ref[0, h : h + 1, :], stats_ref[1, h : h + 1, :], summed_ref[head, :])
        for h, head in enumerate(heads)
    )
    for column, pair_ref, seg_ref in ((0, before_ref, before_seg_ref), (4, after_ref, after_seg_ref)):
        state = lax.fori_loop(
            bounds[block, column],
            bounds[block, column + 1],
            functools.partial(
                attend_step,
                [(pair_ref, head) for head in heads],
                seg_ref,
                query_seg_ref[...],
                queries,
            ),
            state,
        )
    rows = pl.ds(pl.multiple_of(block * QUERY_BLOCK, QUERY_BLOCK), QUERY_BLOCK)
    for head, (peak, total, summed) in zip(heads, state):
        attended_ref[rows, head] = (summed * (1.0 / total)).T.astype(jnp.bfloat16)

    @pl.when(block == pl.num_programs(0) - 1)
    def _():
        out_ref[...] = jnp.dot(
            place_ref[...], attended_ref[...], preferred_element_type=jnp.float32
        ).astype(jnp.bfloat16)


def whole(*shape):
    return pl.BlockSpec(shape, lambda i, b: (0,) * len(shape))


def at_column(shape, column):
    return pl.BlockSpec(shape, lambda i, b: (0,) * (len(shape) - 1) + (column,))


def query_rows(width, column):
    return pl.BlockSpec((QUERY_BLOCK, width), lambda i, b: (i, column))


def query_lanes(*shape):
    return pl.BlockSpec(shape + (QUERY_BLOCK,), lambda i, b: (0,) * len(shape) + (i,))


def attend_local(queries, pairs, quarters, query_seg, bounds):
    row_count, width = queries.shape
    quarter = width // 4
    head_count = width // (2 * HEAD)
    return pl.pallas_call(
        local_kernel,
        out_shape=(
            jax.ShapeDtypeStruct((2 * quarter, row_count), jnp.float32),
            jax.ShapeDtypeStruct((2, head_count, row_count), jnp.float32),
        ),
        grid_spec=pltpu.PrefetchScalarGridSpec(
            num_scalar_prefetch=1,
            grid=(row_count // QUERY_BLOCK,),
            in_specs=[query_rows(quarter, q) for q in quarters]
            + [at_column((2, row_count, quarter), q) for q in quarters]
            + [query_lanes(1), whole(row_count, 1)],
            out_specs=[query_lanes(2 * quarter), query_lanes(2, head_count)],
        ),
        compiler_params=pltpu.CompilerParams(vmem_limit_bytes=48 << 20),
        cost_estimate=pl.CostEstimate(
            flops=LOCAL_FLOPS_HINT, transcendentals=1 << 20, bytes_accessed=1 << 22
        ),
        name="attend_local",
    )(bounds, queries, queries, pairs, pairs, query_seg[None, :], query_seg[:, None])


def attend_halo(queries, halo, quarters, query_seg, margin_seg, bounds, local, placement):
    row_count, width = queries.shape
    quarter = width // 4
    head_count = width // (2 * HEAD)
    slot_count = placement.shape[0]
    return pl.pallas_call(
        halo_kernel,
        out_shape=jax.ShapeDtypeStruct((slot_count, 2 * quarter), jnp.bfloat16),
        grid_spec=pltpu.PrefetchScalarGridSpec(
            num_scalar_prefetch=1,
            grid=(row_count // QUERY_BLOCK,),
            in_specs=[query_rows(quarter, q) for q in quarters]
            + [whole(2, SEG_MAX, 2 * quarter)] * 2
            + [
                query_lanes(1),
                whole(SEG_MAX, 1),
                whole(SEG_MAX, 1),
                query_lanes(2 * quarter),
                query_lanes(2, head_count),
                whole(slot_count, row_count),
            ],
            out_specs=whole(slot_count, 2 * quarter),
            scratch_shapes=[pltpu.VMEM((row_count, 2 * quarter), jnp.bfloat16)],
        ),
        compiler_params=pltpu.CompilerParams(vmem_limit_bytes=48 << 20),
        cost_estimate=pl.CostEstimate(
            flops=HALO_FLOPS_HINT, transcendentals=1 << 20, bytes_accessed=1 << 22
        ),
        name="attend_halo",
    )(
        bounds, queries, queries, *halo, query_seg[None, :], margin_seg[:SEG_MAX, None],
        margin_seg[SEG_MAX + row_count :, None], *local, placement,
    )


def key_ranges(segment_ids, query_seg, first_row):
    row_count = query_seg.shape[0]
    firsts = query_seg[::QUERY_BLOCK]
    lasts = query_seg[QUERY_BLOCK - 1 :: QUERY_BLOCK]
    low = jnp.sum((segment_ids[None, :] < firsts[:, None]).astype(jnp.int32), axis=1)
    high = jnp.sum((segment_ids[None, :] <= lasts[:, None]).astype(jnp.int32), axis=1)
    columns = []
    for start, length in ((-SEG_MAX, SEG_MAX), (0, row_count), (row_count, SEG_MAX)):
        part_low = jnp.clip(low - first_row - start, 0, length)
        part_high = jnp.clip(high - first_row - start, 0, length)
        columns += [part_low // KEY_BLOCK, (part_high + KEY_BLOCK - 1) // KEY_BLOCK]
    return jnp.stack(columns, axis=1)


def body(
    queries, keys_values, segment_ids, route_shard, route_slot, control_proj, base_hidden, cotangent
):
    row_count = queries.shape[0]
    width = queries.shape[1]
    model_width = control_proj.shape[1]
    shard_count = lax.axis_size("seq")
    shard_index = lax.axis_index("seq")
    capacity = 2 * row_count // shard_count
    slot_count = shard_count * capacity
    block_rows = width // shard_count
    far_count = shard_count // 4
    core = shard_index % 2
    near = (shard_index // 2) % 2
    far = shard_index // 4
    quarter = width // 4
    far_quarter = far_count // 4

    def swap(value, bit):
        return lax.ppermute(value, "seq", [(i, i ^ bit) for i in range(shard_count)])

    def outer(value):
        return jnp.concatenate([value[..., :quarter], value[..., 3 * quarter :]], axis=-1)

    def inner(value):
        return value[..., quarter : 3 * quarter]

    up = [(i, i + 1) for i in range(shard_count - 1)]
    down = [(j, i) for i, j in up]

    def halo(pairs):
        before = lax.ppermute(pairs[:, row_count - SEG_MAX :], "seq", up)
        after = lax.ppermute(pairs[:, :SEG_MAX], "seq", down)
        return before, after

    first_halo = halo(outer(keys_values))
    gated, first_halo = lax.optimization_barrier((inner(keys_values), first_halo))
    second_halo = halo(gated)
    peer_cotangent = swap(cotangent, 1)

    target_shard = route_shard[:, 0]
    one_hot = (target_shard[:, None] == jnp.arange(shard_count, dtype=jnp.int32)[None, :]).astype(
        jnp.int32
    )
    slot_rank = jnp.sum((jnp.cumsum(one_hot, axis=0) - 1) * one_hot, axis=1)
    flat_place = target_shard * capacity + slot_rank
    place_mask = flat_place[None, :] == jnp.arange(slot_count, dtype=jnp.int32)[:, None]
    placement = place_mask.astype(jnp.bfloat16)
    occupied = jnp.sum(place_mask.astype(jnp.int32), axis=1)
    slot_values = jnp.sum(jnp.where(place_mask, route_slot[None, :], 0), axis=1)
    slot_table = jnp.where(occupied > 0, slot_values, -1).reshape(shard_count, capacity)
    incoming_slots = lax.all_to_all(slot_table, "seq", split_axis=0, concat_axis=0, tiled=True)
    landing = (
        incoming_slots.reshape(-1)[:, None] == jnp.arange(row_count, dtype=jnp.int32)[None, :]
    ).astype(jnp.bfloat16)

    first_row = shard_index * row_count
    query_seg = lax.dynamic_slice_in_dim(segment_ids, first_row, row_count)
    padded_seg = jnp.pad(segment_ids, (SEG_MAX, SEG_MAX), constant_values=-1)
    key_seg = lax.dynamic_slice_in_dim(padded_seg, first_row, row_count + 2 * SEG_MAX)
    bounds = key_ranges(segment_ids, query_seg, first_row)
    quarters = ((0, 3), (1, 2))
    outer_local = attend_local(queries, keys_values, quarters[0], query_seg, bounds)
    inner_local = attend_local(queries, keys_values, quarters[1], query_seg, bounds)
    outer_local, inner_local, first_halo = lax.optimization_barrier(
        (outer_local, inner_local, first_halo)
    )
    outer_placed = attend_halo(
        queries, first_halo, quarters[0], query_seg, key_seg, bounds, outer_local, placement
    )
    inner_placed = attend_halo(
        queries, second_halo, quarters[1], query_seg, key_seg, bounds, inner_local, placement
    )

    def split_columns(parts):
        step = model_width // parts
        return [slice(part * step, (part + 1) * step) for part in range(parts)]

    def product(halves, columns):
        return sum(
            jnp.einsum("fbt,td->fbd", half, other[:, columns], preferred_element_type=jnp.float32)
            for half, other in zip(halves, (cotangent, peer_cotangent))
        )

    def land(value):
        incoming = lax.all_to_all(
            value.reshape(shard_count, capacity, 2 * quarter),
            "seq",
            split_axis=0,
            concat_axis=0,
            tiled=True,
        )
        return jnp.einsum(
            "sk,sr->kr",
            incoming.reshape(slot_count, 2 * quarter),
            landing,
            preferred_element_type=jnp.float32,
        ).astype(jnp.bfloat16)

    def near_reduce(rows, parts):
        by_core = rows.reshape(far_count, 2, block_rows, row_count)
        peer_rows = swap(lax.dynamic_index_in_dim(by_core, 1 - core, 1, keepdims=False), 1)
        own_rows = lax.dynamic_index_in_dim(by_core, core, 1, keepdims=False)
        by_near = [
            value.reshape(far_count // 2, 2, block_rows, row_count) for value in (own_rows, peer_rows)
        ]
        sent_rows = [lax.dynamic_index_in_dim(v, 1 - near, 1, keepdims=False) for v in by_near]
        kept_rows = [lax.dynamic_index_in_dim(v, near, 1, keepdims=False) for v in by_near]
        sent = [product(sent_rows, columns).astype(jnp.bfloat16) for columns in split_columns(parts)]
        summed = [
            product(kept_rows, columns) + swap(value, 2).astype(jnp.float32)
            for columns, value in zip(split_columns(parts), sent)
        ]
        return sent, summed

    def far_exchange(chunk, summed):
        members = [
            f for f in range(far_count) if (far_quarter <= f < 3 * far_quarter) == (chunk == 1)
        ]

        def place_of(index):
            if chunk == 1:
                return index - far_quarter
            return jnp.where(index < far_quarter, index, index - 2 * far_quarter)

        kept = lax.dynamic_index_in_dim(summed, place_of(far), 0, keepdims=False)
        rounded = summed.astype(jnp.bfloat16)
        arrived = []
        for other in range(1, far_count):
            piece = lax.dynamic_index_in_dim(rounded, place_of(far ^ other), 0, keepdims=False)
            routes = [
                (i, i ^ (4 * other)) for i in range(shard_count) if (i // 4) ^ other in members
            ]
            arrived.append(lax.ppermute(piece, "seq", routes))
        return kept, arrived

    def far_total(kept, arrived):
        return kept + sum(value.astype(jnp.float32) for value in arrived)

    outer_rows = land(outer_placed)
    _, outer_summed = near_reduce(outer_rows, OUTER_PARTS)
    outer_far = [far_exchange(0, value) for value in outer_summed]
    inner_rows = land(inner_placed)
    _, inner_summed = near_reduce(inner_rows, INNER_PARTS)
    outer_far, late_rows, inner_summed[0] = lax.optimization_barrier(
        (outer_far, inner_rows, inner_summed[0])
    )
    inner_far = [far_exchange(1, value) for value in inner_summed]
    grad_parts = [
        jnp.concatenate([far_total(*pair) for pair in pairs], axis=1)
        for pairs in (outer_far, inner_far)
    ]
    in_middle = (far >= far_quarter) & (far < 3 * far_quarter)
    proj_grad = jnp.where(in_middle, grad_parts[1], grad_parts[0])

    added = jnp.einsum(
        "kr,kd->rd",
        jnp.concatenate([outer_rows[:quarter], late_rows, outer_rows[quarter:]], axis=0),
        control_proj,
        preferred_element_type=jnp.float32,
    )
    mixed_hidden = (base_hidden.astype(jnp.float32) + added).astype(jnp.bfloat16)
    return (mixed_hidden, proj_grad)


def solution(mesh):
    placed = (
        P(("grp", "seq"), None),
        P(None, ("grp", "seq"), None),
        P("grp"),
        P(("grp", "seq"), None),
        P(("grp", "seq")),
        P(),
        P(("grp", "seq"), None),
        P(("grp", "seq"), None),
    )
    return jax.shard_map(
        body,
        mesh=mesh,
        in_specs=placed,
        out_specs=(P(("grp", "seq"), None), P(("grp", "seq"), None)),
        check_vma=False,
    )
```

```python
import functools
import math

import jax
import jax.numpy as jnp
from jax import lax
from jax.experimental import pallas as pl
from jax.experimental.pallas import tpu as pltpu
from jax.sharding import PartitionSpec as P

HEAD = 128
SEG_MAX = 512
QUERY_BLOCK = 128
KEY_BLOCK = 256
OUTER_PARTS = 2
INNER_PARTS = 2
LOCAL_FLOPS_HINT = 1 << 33
HALO_FLOPS_HINT = 1 << 34
MASKED = -1e30
EXP2_SCALE = HEAD ** (-0.5) * math.log2(math.e)


def attend_step(pairs, key_seg_ref, query_seg, queries, key_block, state):
    offset = pl.multiple_of(key_block * KEY_BLOCK, KEY_BLOCK)
    keep = key_seg_ref[pl.ds(offset, KEY_BLOCK), :] == query_seg
    result = []
    for (pair_ref, head), query, (peak, total, summed) in zip(pairs, queries, state):
        keys = pair_ref[0, pl.ds(offset, KEY_BLOCK), head]
        values = pair_ref[1, pl.ds(offset, KEY_BLOCK), head]
        scores = lax.dot_general(
            keys, query, (((1,), (1,)), ((), ())), preferred_element_type=jnp.float32
        )
        scores = jnp.where(keep, scores, MASKED)
        new_peak = jnp.maximum(peak, jnp.max(scores, axis=0, keepdims=True))
        weights = jnp.exp2((scores - new_peak) * EXP2_SCALE)
        shrink = jnp.exp2((peak - new_peak) * EXP2_SCALE)
        total = total * shrink + jnp.sum(weights, axis=0, keepdims=True)
        summed = summed * shrink + lax.dot_general(
            values,
            weights.astype(jnp.bfloat16),
            (((0,), (0,)), ((), ())),
            preferred_element_type=jnp.float32,
        )
        result.append((new_peak, total, summed))
    return tuple(result)


def head_slices(width):
    return [slice(start, start + HEAD) for start in range(0, width, HEAD)]


def local_kernel(
    bounds, first_query_ref, last_query_ref, first_own_ref, last_own_ref, query_seg_ref,
    key_seg_ref, summed_ref, stats_ref,
):
    block = pl.program_id(0)
    heads = head_slices(first_query_ref.shape[1])
    state = tuple(
        (
            jnp.full((1, QUERY_BLOCK), MASKED, jnp.float32),
            jnp.zeros((1, QUERY_BLOCK), jnp.float32),
            jnp.zeros((HEAD, QUERY_BLOCK), jnp.float32),
        )
        for _ in range(2 * len(heads))
    )
    state = lax.fori_loop(
        bounds[block, 2],
        bounds[block, 3],
        functools.partial(
            attend_step,
            [(ref, head) for ref in (first_own_ref, last_own_ref) for head in heads],
            key_seg_ref,
            query_seg_ref[...],
            [ref[:, head] for ref in (first_query_ref, last_query_ref) for head in heads],
        ),
        state,
    )
    for h, (peak, total, summed) in enumerate(state):
        stats_ref[0, h : h + 1, :] = peak
        stats_ref[1, h : h + 1, :] = total
        summed_ref[h * HEAD : (h + 1) * HEAD, :] = summed


def halo_kernel(
    bounds, first_query_ref, last_query_ref, before_ref, after_ref, query_seg_ref,
    before_seg_ref, after_seg_ref, summed_ref, stats_ref, place_ref, out_ref, attended_ref,
):
    block = pl.program_id(0)
    half_width = first_query_ref.shape[1]
    heads = head_slices(2 * half_width)
    queries = [
        ref[:, head] for ref in (first_query_ref, last_query_ref) for head in head_slices(half_width)
    ]
    state = tuple(
        (stats_ref[0, h : h + 1, :], stats_ref[1, h : h + 1, :], summed_ref[head, :])
        for h, head in enumerate(heads)
    )
    for column, pair_ref, seg_ref in ((0, before_ref, before_seg_ref), (4, after_ref, after_seg_ref)):
        state = lax.fori_loop(
            bounds[block, column],
            bounds[block, column + 1],
            functools.partial(
                attend_step,
                [(pair_ref, head) for head in heads],
                seg_ref,
                query_seg_ref[...],
                queries,
            ),
            state,
        )
    rows = pl.ds(pl.multiple_of(block * QUERY_BLOCK, QUERY_BLOCK), QUERY_BLOCK)
    for head, (peak, total, summed) in zip(heads, state):
        attended_ref[rows, head] = (summed * (1.0 / total)).T.astype(jnp.bfloat16)

    @pl.when(block == pl.num_programs(0) - 1)
    def _():
        out_ref[...] = jnp.dot(
            place_ref[...], attended_ref[...], preferred_element_type=jnp.float32
        ).astype(jnp.bfloat16)


def whole(*shape):
    return pl.BlockSpec(shape, lambda i, b: (0,) * len(shape))


def at_column(shape, column):
    return pl.BlockSpec(shape, lambda i, b: (0,) * (len(shape) - 1) + (column,))


def query_rows(width, column):
    return pl.BlockSpec((QUERY_BLOCK, width), lambda i, b: (i, column))


def query_lanes(*shape):
    return pl.BlockSpec(shape + (QUERY_BLOCK,), lambda i, b: (0,) * len(shape) + (i,))


def attend_local(queries, pairs, quarters, query_seg, bounds):
    row_count, width = queries.shape
    quarter = width // 4
    head_count = width // (2 * HEAD)
    return pl.pallas_call(
        local_kernel,
        out_shape=(
            jax.ShapeDtypeStruct((2 * quarter, row_count), jnp.float32),
            jax.ShapeDtypeStruct((2, head_count, row_count), jnp.float32),
        ),
        grid_spec=pltpu.PrefetchScalarGridSpec(
            num_scalar_prefetch=1,
            grid=(row_count // QUERY_BLOCK,),
            in_specs=[query_rows(quarter, q) for q in quarters]
            + [at_column((2, row_count, quarter), q) for q in quarters]
            + [query_lanes(1), whole(row_count, 1)],
            out_specs=[query_lanes(2 * quarter), query_lanes(2, head_count)],
        ),
        compiler_params=pltpu.CompilerParams(vmem_limit_bytes=48 << 20),
        cost_estimate=pl.CostEstimate(
            flops=LOCAL_FLOPS_HINT, transcendentals=1 << 20, bytes_accessed=1 << 22
        ),
        name="attend_local",
    )(bounds, queries, queries, pairs, pairs, query_seg[None, :], query_seg[:, None])


def attend_halo(queries, halo, quarters, query_seg, margin_seg, bounds, local, placement):
    row_count, width = queries.shape
    quarter = width // 4
    head_count = width // (2 * HEAD)
    slot_count = placement.shape[0]
    return pl.pallas_call(
        halo_kernel,
        out_shape=jax.ShapeDtypeStruct((slot_count, 2 * quarter), jnp.bfloat16),
        grid_spec=pltpu.PrefetchScalarGridSpec(
            num_scalar_prefetch=1,
            grid=(row_count // QUERY_BLOCK,),
            in_specs=[query_rows(quarter, q) for q in quarters]
            + [whole(2, SEG_MAX, 2 * quarter)] * 2
            + [
                query_lanes(1),
                whole(SEG_MAX, 1),
                whole(SEG_MAX, 1),
                query_lanes(2 * quarter),
                query_lanes(2, head_count),
                whole(slot_count, row_count),
            ],
            out_specs=whole(slot_count, 2 * quarter),
            scratch_shapes=[pltpu.VMEM((row_count, 2 * quarter), jnp.bfloat16)],
        ),
        compiler_params=pltpu.CompilerParams(vmem_limit_bytes=48 << 20),
        cost_estimate=pl.CostEstimate(
            flops=HALO_FLOPS_HINT, transcendentals=1 << 20, bytes_accessed=1 << 22
        ),
        name="attend_halo",
    )(
        bounds, queries, queries, *halo, query_seg[None, :], margin_seg[:SEG_MAX, None],
        margin_seg[SEG_MAX + row_count :, None], *local, placement,
    )


def key_ranges(segment_ids, query_seg, first_row):
    row_count = query_seg.shape[0]
    firsts = query_seg[::QUERY_BLOCK]
    lasts = query_seg[QUERY_BLOCK - 1 :: QUERY_BLOCK]
    low = jnp.sum((segment_ids[None, :] < firsts[:, None]).astype(jnp.int32), axis=1)
    high = jnp.sum((segment_ids[None, :] <= lasts[:, None]).astype(jnp.int32), axis=1)
    columns = []
    for start, length in ((-SEG_MAX, SEG_MAX), (0, row_count), (row_count, SEG_MAX)):
        part_low = jnp.clip(low - first_row - start, 0, length)
        part_high = jnp.clip(high - first_row - start, 0, length)
        columns += [part_low // KEY_BLOCK, (part_high + KEY_BLOCK - 1) // KEY_BLOCK]
    return jnp.stack(columns, axis=1)


def body(
    queries, keys_values, segment_ids, route_shard, route_slot, control_proj, base_hidden, cotangent
):
    row_count = queries.shape[0]
    width = queries.shape[1]
    model_width = control_proj.shape[1]
    shard_count = lax.axis_size("seq")
    shard_index = lax.axis_index("seq")
    capacity = 2 * row_count // shard_count
    slot_count = shard_count * capacity
    block_rows = width // shard_count
    far_count = shard_count // 4
    core = shard_index % 2
    near = (shard_index // 2) % 2
    far = shard_index // 4
    quarter = width // 4
    far_quarter = far_count // 4

    def swap(value, bit):
        return lax.ppermute(value, "seq", [(i, i ^ bit) for i in range(shard_count)])

    def outer(value):
        return jnp.concatenate([value[..., :quarter], value[..., 3 * quarter :]], axis=-1)

    def inner(value):
        return value[..., quarter : 3 * quarter]

    up = [(i, i + 1) for i in range(shard_count - 1)]
    down = [(j, i) for i, j in up]

    def halo(pairs):
        before = lax.ppermute(pairs[:, row_count - SEG_MAX :], "seq", up)
        after = lax.ppermute(pairs[:, :SEG_MAX], "seq", down)
        return before, after

    first_halo = halo(outer(keys_values))
    gated, first_halo = lax.optimization_barrier((inner(keys_values), first_halo))
    second_halo = halo(gated)
    peer_cotangent = swap(cotangent, 1)

    target_shard = route_shard[:, 0]
    one_hot = (target_shard[:, None] == jnp.arange(shard_count, dtype=jnp.int32)[None, :]).astype(
        jnp.int32
    )
    slot_rank = jnp.sum((jnp.cumsum(one_hot, axis=0) - 1) * one_hot, axis=1)
    flat_place = target_shard * capacity + slot_rank
    place_mask = flat_place[None, :] == jnp.arange(slot_count, dtype=jnp.int32)[:, None]
    placement = place_mask.astype(jnp.bfloat16)
    occupied = jnp.sum(place_mask.astype(jnp.int32), axis=1)
    slot_values = jnp.sum(jnp.where(place_mask, route_slot[None, :], 0), axis=1)
    slot_table = jnp.where(occupied > 0, slot_values, -1).reshape(shard_count, capacity)
    incoming_slots = lax.all_to_all(slot_table, "seq", split_axis=0, concat_axis=0, tiled=True)
    landing = (
        incoming_slots.reshape(-1)[:, None] == jnp.arange(row_count, dtype=jnp.int32)[None, :]
    ).astype(jnp.bfloat16)

    first_row = shard_index * row_count
    query_seg = lax.dynamic_slice_in_dim(segment_ids, first_row, row_count)
    padded_seg = jnp.pad(segment_ids, (SEG_MAX, SEG_MAX), constant_values=-1)
    key_seg = lax.dynamic_slice_in_dim(padded_seg, first_row, row_count + 2 * SEG_MAX)
    bounds = key_ranges(segment_ids, query_seg, first_row)
    quarters = ((0, 3), (1, 2))
    outer_local = attend_local(queries, keys_values, quarters[0], query_seg, bounds)
    inner_local = attend_local(queries, keys_values, quarters[1], query_seg, bounds)
    outer_local, inner_local, first_halo = lax.optimization_barrier(
        (outer_local, inner_local, first_halo)
    )
    outer_placed = attend_halo(
        queries, first_halo, quarters[0], query_seg, key_seg, bounds, outer_local, placement
    )
    inner_placed = attend_halo(
        queries, second_halo, quarters[1], query_seg, key_seg, bounds, inner_local, placement
    )

    def split_columns(parts):
        step = model_width // parts
        return [slice(part * step, (part + 1) * step) for part in range(parts)]

    def product(halves, columns):
        return sum(
            jnp.einsum("fbt,td->fbd", half, other[:, columns], preferred_element_type=jnp.float32)
            for half, other in zip(halves, (cotangent, peer_cotangent))
        )

    def land(value):
        incoming = lax.all_to_all(
            value.reshape(shard_count, capacity, 2 * quarter),
            "seq",
            split_axis=0,
            concat_axis=0,
            tiled=True,
        )
        return jnp.einsum(
            "sk,sr->kr",
            incoming.reshape(slot_count, 2 * quarter),
            landing,
            preferred_element_type=jnp.float32,
        ).astype(jnp.bfloat16)

    def near_parts(rows):
        by_core = rows.reshape(far_count, 2, block_rows, row_count)
        peer_rows = swap(lax.dynamic_index_in_dim(by_core, 1 - core, 1, keepdims=False), 1)
        own_rows = lax.dynamic_index_in_dim(by_core, core, 1, keepdims=False)
        by_near = [
            value.reshape(far_count // 2, 2, block_rows, row_count) for value in (own_rows, peer_rows)
        ]
        return [
            [lax.dynamic_index_in_dim(v, which, 1, keepdims=False) for v in by_near]
            for which in (1 - near, near)
        ]

    def near_exchange(sent_rows, parts):
        sent = [product(sent_rows, columns).astype(jnp.bfloat16) for columns in split_columns(parts)]
        return sent, [swap(value, 2) for value in sent]

    def near_sum(kept_rows, arrived):
        return [
            product(kept_rows, columns) + value.astype(jnp.float32)
            for columns, value in zip(split_columns(len(arrived)), arrived)
        ]

    def line_exchange(chunk, summed, rounded):
        def pick(value, holder):
            return lax.dynamic_index_in_dim(
                value, jnp.where(far == holder, 1, 0), 0, keepdims=False
            )

        def hop(piece, moves):
            routes = [(4 * a + i, 4 * b + i) for a, b in moves for i in range(4)]
            return lax.ppermute(piece, "seq", routes)

        def add(holder, arrived):
            return (pick(summed, holder) + arrived.astype(jnp.float32)).astype(jnp.bfloat16)

        inward = hop(pick(rounded, 0), ((0, 1), (3, 2)))
        across = hop(add(1, inward), ((1, 2), (2, 1)))
        if chunk == 0:
            return [hop(add(2, across), ((2, 3), (1, 0)))]
        return [hop(pick(rounded, 3), ((0, 1), (3, 2))), across]

    def far_exchange(chunk, summed, rounded):
        members = [
            f for f in range(far_count) if (far_quarter <= f < 3 * far_quarter) == (chunk == 1)
        ]

        def place_of(index):
            if chunk == 1:
                return index - far_quarter
            return jnp.where(index < far_quarter, index, index - 2 * far_quarter)

        kept = lax.dynamic_index_in_dim(summed, place_of(far), 0, keepdims=False)
        if far_count == 4 and chunk == 1:
            return kept, line_exchange(chunk, summed, rounded)
        arrived = []
        for other in range(1, far_count):
            piece = lax.dynamic_index_in_dim(rounded, place_of(far ^ other), 0, keepdims=False)
            routes = [
                (i, i ^ (4 * other)) for i in range(shard_count) if (i // 4) ^ other in members
            ]
            arrived.append(lax.ppermute(piece, "seq", routes))
        return kept, arrived

    def far_total(kept, arrived):
        return kept + sum(value.astype(jnp.float32) for value in arrived)

    outer_rows = land(outer_placed)
    outer_sent_rows, outer_kept_rows = near_parts(outer_rows)
    _, outer_arrived = near_exchange(outer_sent_rows, OUTER_PARTS)
    inner_rows = land(inner_placed)
    inner_sent_rows, inner_kept_rows = near_parts(inner_rows)
    inner_sent, inner_arrived = near_exchange(inner_sent_rows, INNER_PARTS)
    outer_arrived[1], _ = lax.optimization_barrier((outer_arrived[1], inner_rows))
    outer_summed = near_sum(outer_kept_rows, outer_arrived)
    outer_far = [far_exchange(0, value, value.astype(jnp.bfloat16)) for value in outer_summed]
    inner_summed = near_sum(inner_kept_rows, inner_arrived)
    inner_rounded = [value.astype(jnp.bfloat16) for value in inner_summed]
    outer_far[0], _ = lax.optimization_barrier((outer_far[0], inner_sent))
    outer_far[1], _ = lax.optimization_barrier((outer_far[1], inner_rounded[0]))
    late_rows, _ = lax.optimization_barrier((inner_rows, inner_sent))
    inner_far = [far_exchange(1, *pair) for pair in zip(inner_summed, inner_rounded)]
    grad_parts = [
        jnp.concatenate([far_total(*pair) for pair in pairs], axis=1)
        for pairs in (outer_far, inner_far)
    ]
    in_middle = (far >= far_quarter) & (far < 3 * far_quarter)
    proj_grad = jnp.where(in_middle, grad_parts[1], grad_parts[0])

    added = jnp.einsum(
        "kr,kd->rd",
        jnp.concatenate([outer_rows[:quarter], late_rows, outer_rows[quarter:]], axis=0),
        control_proj,
        preferred_element_type=jnp.float32,
    )
    mixed_hidden = (base_hidden.astype(jnp.float32) + added).astype(jnp.bfloat16)
    return (mixed_hidden, proj_grad)


def solution(mesh):
    placed = (
        P(("grp", "seq"), None),
        P(None, ("grp", "seq"), None),
        P("grp"),
        P(("grp", "seq"), None),
        P(("grp", "seq")),
        P(),
        P(("grp", "seq"), None),
        P(("grp", "seq"), None),
    )
    return jax.shard_map(
        body,
        mesh=mesh,
        in_specs=placed,
        out_specs=(P(("grp", "seq"), None), P(("grp", "seq"), None)),
        check_vma=False,
    )
```

```python
import functools
import math

import jax
import jax.numpy as jnp
from jax import lax
from jax.experimental import pallas as pl
from jax.experimental.pallas import tpu as pltpu
from jax.sharding import PartitionSpec as P

HEAD = 128
SEG_MAX = 512
QUERY_BLOCK = 128
KEY_BLOCK = 256
OUTER_PARTS = 2
INNER_PARTS = 2
LOCAL_FLOPS_HINT = 1 << 33
HALO_FLOPS_HINT = 1 << 34
MASKED = -1e30
EXP2_SCALE = HEAD ** (-0.5) * math.log2(math.e)


def attend_step(pairs, key_seg_ref, query_seg, queries, key_block, state):
    offset = pl.multiple_of(key_block * KEY_BLOCK, KEY_BLOCK)
    keep = key_seg_ref[pl.ds(offset, KEY_BLOCK), :] == query_seg
    result = []
    for (pair_ref, head), query, (peak, total, summed) in zip(pairs, queries, state):
        keys = pair_ref[0, pl.ds(offset, KEY_BLOCK), head]
        values = pair_ref[1, pl.ds(offset, KEY_BLOCK), head]
        scores = lax.dot_general(
            keys, query, (((1,), (1,)), ((), ())), preferred_element_type=jnp.float32
        )
        scores = jnp.where(keep, scores, MASKED)
        new_peak = jnp.maximum(peak, jnp.max(scores, axis=0, keepdims=True))
        weights = jnp.exp2((scores - new_peak) * EXP2_SCALE)
        shrink = jnp.exp2((peak - new_peak) * EXP2_SCALE)
        total = total * shrink + jnp.sum(weights, axis=0, keepdims=True)
        summed = summed * shrink + lax.dot_general(
            values,
            weights.astype(jnp.bfloat16),
            (((0,), (0,)), ((), ())),
            preferred_element_type=jnp.float32,
        )
        result.append((new_peak, total, summed))
    return tuple(result)


def head_slices(width):
    return [slice(start, start + HEAD) for start in range(0, width, HEAD)]


def local_kernel(
    bounds, first_query_ref, last_query_ref, first_own_ref, last_own_ref, query_seg_ref,
    key_seg_ref, summed_ref, stats_ref,
):
    block = pl.program_id(0)
    heads = head_slices(first_query_ref.shape[1])
    state = tuple(
        (
            jnp.full((1, QUERY_BLOCK), MASKED, jnp.float32),
            jnp.zeros((1, QUERY_BLOCK), jnp.float32),
            jnp.zeros((HEAD, QUERY_BLOCK), jnp.float32),
        )
        for _ in range(2 * len(heads))
    )
    state = lax.fori_loop(
        bounds[block, 2],
        bounds[block, 3],
        functools.partial(
            attend_step,
            [(ref, head) for ref in (first_own_ref, last_own_ref) for head in heads],
            key_seg_ref,
            query_seg_ref[...],
            [ref[:, head] for ref in (first_query_ref, last_query_ref) for head in heads],
        ),
        state,
    )
    for h, (peak, total, summed) in enumerate(state):
        stats_ref[0, h : h + 1, :] = peak
        stats_ref[1, h : h + 1, :] = total
        summed_ref[h * HEAD : (h + 1) * HEAD, :] = summed


def halo_kernel(
    bounds, first_query_ref, last_query_ref, before_ref, after_ref, query_seg_ref,
    before_seg_ref, after_seg_ref, summed_ref, stats_ref, place_ref, out_ref, attended_ref,
):
    block = pl.program_id(0)
    half_width = first_query_ref.shape[1]
    heads = head_slices(2 * half_width)
    queries = [
        ref[:, head] for ref in (first_query_ref, last_query_ref) for head in head_slices(half_width)
    ]
    state = tuple(
        (stats_ref[0, h : h + 1, :], stats_ref[1, h : h + 1, :], summed_ref[head, :])
        for h, head in enumerate(heads)
    )
    for column, pair_ref, seg_ref in ((0, before_ref, before_seg_ref), (4, after_ref, after_seg_ref)):
        state = lax.fori_loop(
            bounds[block, column],
            bounds[block, column + 1],
            functools.partial(
                attend_step,
                [(pair_ref, head) for head in heads],
                seg_ref,
                query_seg_ref[...],
                queries,
            ),
            state,
        )
    rows = pl.ds(pl.multiple_of(block * QUERY_BLOCK, QUERY_BLOCK), QUERY_BLOCK)
    for head, (peak, total, summed) in zip(heads, state):
        attended_ref[rows, head] = (summed * (1.0 / total)).T.astype(jnp.bfloat16)

    @pl.when(block == pl.num_programs(0) - 1)
    def _():
        out_ref[...] = jnp.dot(
            place_ref[...], attended_ref[...], preferred_element_type=jnp.float32
        ).astype(jnp.bfloat16)


def whole(*shape):
    return pl.BlockSpec(shape, lambda i, b: (0,) * len(shape))


def at_column(shape, column):
    return pl.BlockSpec(shape, lambda i, b: (0,) * (len(shape) - 1) + (column,))


def query_rows(width, column):
    return pl.BlockSpec((QUERY_BLOCK, width), lambda i, b: (i, column))


def query_lanes(*shape):
    return pl.BlockSpec(shape + (QUERY_BLOCK,), lambda i, b: (0,) * len(shape) + (i,))


def attend_local(queries, pairs, quarters, query_seg, bounds):
    row_count, width = queries.shape
    quarter = width // 4
    head_count = width // (2 * HEAD)
    return pl.pallas_call(
        local_kernel,
        out_shape=(
            jax.ShapeDtypeStruct((2 * quarter, row_count), jnp.float32),
            jax.ShapeDtypeStruct((2, head_count, row_count), jnp.float32),
        ),
        grid_spec=pltpu.PrefetchScalarGridSpec(
            num_scalar_prefetch=1,
            grid=(row_count // QUERY_BLOCK,),
            in_specs=[query_rows(quarter, q) for q in quarters]
            + [at_column((2, row_count, quarter), q) for q in quarters]
            + [query_lanes(1), whole(row_count, 1)],
            out_specs=[query_lanes(2 * quarter), query_lanes(2, head_count)],
        ),
        compiler_params=pltpu.CompilerParams(vmem_limit_bytes=48 << 20),
        cost_estimate=pl.CostEstimate(
            flops=LOCAL_FLOPS_HINT, transcendentals=1 << 20, bytes_accessed=1 << 22
        ),
        name="attend_local",
    )(bounds, queries, queries, pairs, pairs, query_seg[None, :], query_seg[:, None])


def attend_halo(queries, halo, quarters, query_seg, margin_seg, bounds, local, placement):
    row_count, width = queries.shape
    quarter = width // 4
    head_count = width // (2 * HEAD)
    slot_count = placement.shape[0]
    return pl.pallas_call(
        halo_kernel,
        out_shape=jax.ShapeDtypeStruct((slot_count, 2 * quarter), jnp.bfloat16),
        grid_spec=pltpu.PrefetchScalarGridSpec(
            num_scalar_prefetch=1,
            grid=(row_count // QUERY_BLOCK,),
            in_specs=[query_rows(quarter, q) for q in quarters]
            + [whole(2, SEG_MAX, 2 * quarter)] * 2
            + [
                query_lanes(1),
                whole(SEG_MAX, 1),
                whole(SEG_MAX, 1),
                query_lanes(2 * quarter),
                query_lanes(2, head_count),
                whole(slot_count, row_count),
            ],
            out_specs=whole(slot_count, 2 * quarter),
            scratch_shapes=[pltpu.VMEM((row_count, 2 * quarter), jnp.bfloat16)],
        ),
        compiler_params=pltpu.CompilerParams(vmem_limit_bytes=48 << 20),
        cost_estimate=pl.CostEstimate(
            flops=HALO_FLOPS_HINT, transcendentals=1 << 20, bytes_accessed=1 << 22
        ),
        name="attend_halo",
    )(
        bounds, queries, queries, *halo, query_seg[None, :], margin_seg[:SEG_MAX, None],
        margin_seg[SEG_MAX + row_count :, None], *local, placement,
    )


def key_ranges(segment_ids, query_seg, first_row):
    row_count = query_seg.shape[0]
    firsts = query_seg[::QUERY_BLOCK]
    lasts = query_seg[QUERY_BLOCK - 1 :: QUERY_BLOCK]
    low = jnp.sum((segment_ids[None, :] < firsts[:, None]).astype(jnp.int32), axis=1)
    high = jnp.sum((segment_ids[None, :] <= lasts[:, None]).astype(jnp.int32), axis=1)
    columns = []
    for start, length in ((-SEG_MAX, SEG_MAX), (0, row_count), (row_count, SEG_MAX)):
        part_low = jnp.clip(low - first_row - start, 0, length)
        part_high = jnp.clip(high - first_row - start, 0, length)
        columns += [part_low // KEY_BLOCK, (part_high + KEY_BLOCK - 1) // KEY_BLOCK]
    return jnp.stack(columns, axis=1)


def body(
    queries, keys_values, segment_ids, route_shard, route_slot, control_proj, base_hidden, cotangent
):
    row_count = queries.shape[0]
    width = queries.shape[1]
    model_width = control_proj.shape[1]
    shard_count = lax.axis_size("seq")
    shard_index = lax.axis_index("seq")
    capacity = 2 * row_count // shard_count
    slot_count = shard_count * capacity
    block_rows = width // shard_count
    far_count = shard_count // 4
    core = shard_index % 2
    near = (shard_index // 2) % 2
    far = shard_index // 4
    quarter = width // 4
    far_quarter = far_count // 4

    def swap(value, bit):
        return lax.ppermute(value, "seq", [(i, i ^ bit) for i in range(shard_count)])

    def outer(value):
        return jnp.concatenate([value[..., :quarter], value[..., 3 * quarter :]], axis=-1)

    def inner(value):
        return value[..., quarter : 3 * quarter]

    up = [(i, i + 1) for i in range(shard_count - 1)]
    down = [(j, i) for i, j in up]

    def halo(pairs):
        before = lax.ppermute(pairs[:, row_count - SEG_MAX :], "seq", up)
        after = lax.ppermute(pairs[:, :SEG_MAX], "seq", down)
        return before, after

    first_halo = halo(outer(keys_values))
    gated, first_halo = lax.optimization_barrier((inner(keys_values), first_halo))
    second_halo = halo(gated)
    peer_cotangent = swap(cotangent, 1)

    target_shard = route_shard[:, 0]
    one_hot = (target_shard[:, None] == jnp.arange(shard_count, dtype=jnp.int32)[None, :]).astype(
        jnp.int32
    )
    slot_rank = jnp.sum((jnp.cumsum(one_hot, axis=0) - 1) * one_hot, axis=1)
    flat_place = target_shard * capacity + slot_rank
    place_mask = flat_place[None, :] == jnp.arange(slot_count, dtype=jnp.int32)[:, None]
    placement = place_mask.astype(jnp.bfloat16)
    occupied = jnp.sum(place_mask.astype(jnp.int32), axis=1)
    slot_values = jnp.sum(jnp.where(place_mask, route_slot[None, :], 0), axis=1)
    slot_table = jnp.where(occupied > 0, slot_values, -1).reshape(shard_count, capacity)
    incoming_slots = lax.all_to_all(slot_table, "seq", split_axis=0, concat_axis=0, tiled=True)
    landing = (
        incoming_slots.reshape(-1)[:, None] == jnp.arange(row_count, dtype=jnp.int32)[None, :]
    ).astype(jnp.bfloat16)

    first_row = shard_index * row_count
    query_seg = lax.dynamic_slice_in_dim(segment_ids, first_row, row_count)
    padded_seg = jnp.pad(segment_ids, (SEG_MAX, SEG_MAX), constant_values=-1)
    key_seg = lax.dynamic_slice_in_dim(padded_seg, first_row, row_count + 2 * SEG_MAX)
    bounds = key_ranges(segment_ids, query_seg, first_row)
    quarters = ((0, 3), (1, 2))
    outer_local = attend_local(queries, keys_values, quarters[0], query_seg, bounds)
    inner_local = attend_local(queries, keys_values, quarters[1], query_seg, bounds)
    outer_local, inner_local, first_halo = lax.optimization_barrier(
        (outer_local, inner_local, first_halo)
    )
    outer_placed = attend_halo(
        queries, first_halo, quarters[0], query_seg, key_seg, bounds, outer_local, placement
    )
    inner_placed = attend_halo(
        queries, second_halo, quarters[1], query_seg, key_seg, bounds, inner_local, placement
    )

    def split_columns(parts):
        step = model_width // parts
        return [slice(part * step, (part + 1) * step) for part in range(parts)]

    def product(halves, columns):
        return sum(
            jnp.einsum("fbt,td->fbd", half, other[:, columns], preferred_element_type=jnp.float32)
            for half, other in zip(halves, (cotangent, peer_cotangent))
        )

    def land(value):
        incoming = lax.all_to_all(
            value.reshape(shard_count, capacity, 2 * quarter),
            "seq",
            split_axis=0,
            concat_axis=0,
            tiled=True,
        )
        return jnp.einsum(
            "sk,sr->kr",
            incoming.reshape(slot_count, 2 * quarter),
            landing,
            preferred_element_type=jnp.float32,
        ).astype(jnp.bfloat16)

    def near_parts(rows):
        by_core = rows.reshape(far_count, 2, block_rows, row_count)
        peer_rows = swap(lax.dynamic_index_in_dim(by_core, 1 - core, 1, keepdims=False), 1)
        own_rows = lax.dynamic_index_in_dim(by_core, core, 1, keepdims=False)
        by_near = [
            value.reshape(far_count // 2, 2, block_rows, row_count) for value in (own_rows, peer_rows)
        ]
        return [
            [lax.dynamic_index_in_dim(v, which, 1, keepdims=False) for v in by_near]
            for which in (1 - near, near)
        ]

    def near_exchange(sent_rows, parts):
        sent = [product(sent_rows, columns).astype(jnp.bfloat16) for columns in split_columns(parts)]
        return sent, [swap(value, 2) for value in sent]

    def near_sum(kept_rows, arrived):
        return [
            product(kept_rows, columns) + value.astype(jnp.float32)
            for columns, value in zip(split_columns(len(arrived)), arrived)
        ]

    def line_exchange(chunk, summed, rounded):
        def pick(value, holder):
            return lax.dynamic_index_in_dim(
                value, jnp.where(far == holder, 1, 0), 0, keepdims=False
            )

        def hop(piece, moves):
            routes = [(4 * a + i, 4 * b + i) for a, b in moves for i in range(4)]
            return lax.ppermute(piece, "seq", routes)

        def add(holder, arrived):
            return (pick(summed, holder) + arrived.astype(jnp.float32)).astype(jnp.bfloat16)

        inward = hop(pick(rounded, 0), ((0, 1), (3, 2)))
        across = hop(add(1, inward), ((1, 2), (2, 1)))
        if chunk == 0:
            return [hop(add(2, across), ((2, 3), (1, 0)))]
        return [hop(pick(rounded, 3), ((0, 1), (3, 2))), across]

    def far_exchange(chunk, summed, rounded):
        members = [
            f for f in range(far_count) if (far_quarter <= f < 3 * far_quarter) == (chunk == 1)
        ]

        def place_of(index):
            if chunk == 1:
                return index - far_quarter
            return jnp.where(index < far_quarter, index, index - 2 * far_quarter)

        kept = lax.dynamic_index_in_dim(summed, place_of(far), 0, keepdims=False)
        if far_count == 4 and chunk == 1:
            return kept, line_exchange(chunk, summed, rounded)
        arrived = []
        for other in range(1, far_count):
            piece = lax.dynamic_index_in_dim(rounded, place_of(far ^ other), 0, keepdims=False)
            routes = [
                (i, i ^ (4 * other)) for i in range(shard_count) if (i // 4) ^ other in members
            ]
            arrived.append(lax.ppermute(piece, "seq", routes))
        return kept, arrived

    def far_total(kept, arrived):
        return kept + sum(value.astype(jnp.float32) for value in arrived)

    outer_rows = land(outer_placed)
    outer_sent_rows, outer_kept_rows = near_parts(outer_rows)
    outer_sent, outer_arrived = near_exchange(outer_sent_rows, OUTER_PARTS)
    early_rows, _ = lax.optimization_barrier((outer_rows, outer_sent))
    def project(rows, weights):
        return jnp.einsum("kr,kd->rd", rows, weights, preferred_element_type=jnp.float32)

    inner_weights = control_proj[quarter : 3 * quarter]
    early_mixed = (
        base_hidden.astype(jnp.float32)
        + project(early_rows[:quarter], control_proj[:quarter])
        + project(early_rows[quarter:], control_proj[3 * quarter :])
    )
    inner_rows = land(inner_placed)
    inner_sent_rows, inner_kept_rows = near_parts(inner_rows)
    inner_sent, inner_arrived = near_exchange(inner_sent_rows, INNER_PARTS)
    outer_arrived[1], _ = lax.optimization_barrier((outer_arrived[1], inner_rows))
    outer_arrived[0], early_mixed = lax.optimization_barrier((outer_arrived[0], early_mixed))
    outer_summed = near_sum(outer_kept_rows, outer_arrived)
    outer_far = [far_exchange(0, value, value.astype(jnp.bfloat16)) for value in outer_summed]
    inner_summed = near_sum(inner_kept_rows, inner_arrived)
    inner_rounded = [value.astype(jnp.bfloat16) for value in inner_summed]
    outer_far[0], _ = lax.optimization_barrier((outer_far[0], inner_sent))
    outer_far[1], _ = lax.optimization_barrier((outer_far[1], inner_rounded[0]))
    late_rows, _ = lax.optimization_barrier((inner_rows, inner_rounded[0]))
    inner_far = [far_exchange(1, *pair) for pair in zip(inner_summed, inner_rounded)]
    grad_parts = [
        jnp.concatenate([far_total(*pair) for pair in pairs], axis=1)
        for pairs in (outer_far, inner_far)
    ]
    in_middle = (far >= far_quarter) & (far < 3 * far_quarter)
    proj_grad = jnp.where(in_middle, grad_parts[1], grad_parts[0])

    mixed_hidden = (early_mixed + project(late_rows, inner_weights)).astype(jnp.bfloat16)
    return (mixed_hidden, proj_grad)


def solution(mesh):
    placed = (
        P(("grp", "seq"), None),
        P(None, ("grp", "seq"), None),
        P("grp"),
        P(("grp", "seq"), None),
        P(("grp", "seq")),
        P(),
        P(("grp", "seq"), None),
        P(("grp", "seq"), None),
    )
    return jax.shard_map(
        body,
        mesh=mesh,
        in_specs=placed,
        out_specs=(P(("grp", "seq"), None), P(("grp", "seq"), None)),
        check_vma=False,
    )
```

```python
import functools
import math

import jax
import jax.numpy as jnp
from jax import lax
from jax.experimental import pallas as pl
from jax.experimental.pallas import tpu as pltpu
from jax.sharding import PartitionSpec as P

HEAD = 128
SEG_MAX = 512
QUERY_BLOCK = 128
KEY_BLOCK = 256
OUTER_PARTS = 2
INNER_PARTS = 2
LOCAL_FLOPS_HINT = 1 << 33
HALO_FLOPS_HINT = 1 << 34
MASKED = -1e30
EXP2_SCALE = HEAD ** (-0.5) * math.log2(math.e)


def attend_step(pairs, key_seg_ref, query_seg, queries, key_block, state):
    offset = pl.multiple_of(key_block * KEY_BLOCK, KEY_BLOCK)
    keep = key_seg_ref[pl.ds(offset, KEY_BLOCK), :] == query_seg
    result = []
    for (pair_ref, head), query, (peak, total, summed) in zip(pairs, queries, state):
        keys = pair_ref[0, pl.ds(offset, KEY_BLOCK), head]
        values = pair_ref[1, pl.ds(offset, KEY_BLOCK), head]
        scores = lax.dot_general(
            keys, query, (((1,), (1,)), ((), ())), preferred_element_type=jnp.float32
        )
        scores = jnp.where(keep, scores, MASKED)
        new_peak = jnp.maximum(peak, jnp.max(scores, axis=0, keepdims=True))
        weights = jnp.exp2((scores - new_peak) * EXP2_SCALE)
        shrink = jnp.exp2((peak - new_peak) * EXP2_SCALE)
        total = total * shrink + jnp.sum(weights, axis=0, keepdims=True)
        summed = summed * shrink + lax.dot_general(
            values,
            weights.astype(jnp.bfloat16),
            (((0,), (0,)), ((), ())),
            preferred_element_type=jnp.float32,
        )
        result.append((new_peak, total, summed))
    return tuple(result)


def head_slices(width):
    return [slice(start, start + HEAD) for start in range(0, width, HEAD)]


def local_kernel(
    bounds, first_query_ref, last_query_ref, first_own_ref, last_own_ref, query_seg_ref,
    key_seg_ref, summed_ref, stats_ref,
):
    block = pl.program_id(0)
    heads = head_slices(first_query_ref.shape[1])
    state = tuple(
        (
            jnp.full((1, QUERY_BLOCK), MASKED, jnp.float32),
            jnp.zeros((1, QUERY_BLOCK), jnp.float32),
            jnp.zeros((HEAD, QUERY_BLOCK), jnp.float32),
        )
        for _ in range(2 * len(heads))
    )
    state = lax.fori_loop(
        bounds[block, 2],
        bounds[block, 3],
        functools.partial(
            attend_step,
            [(ref, head) for ref in (first_own_ref, last_own_ref) for head in heads],
            key_seg_ref,
            query_seg_ref[...],
            [ref[:, head] for ref in (first_query_ref, last_query_ref) for head in heads],
        ),
        state,
    )
    for h, (peak, total, summed) in enumerate(state):
        stats_ref[0, h : h + 1, :] = peak
        stats_ref[1, h : h + 1, :] = total
        summed_ref[h * HEAD : (h + 1) * HEAD, :] = summed


def halo_kernel(
    bounds, first_query_ref, last_query_ref, before_ref, after_ref, query_seg_ref,
    before_seg_ref, after_seg_ref, summed_ref, stats_ref, place_ref, out_ref, attended_ref,
):
    block = pl.program_id(0)
    half_width = first_query_ref.shape[1]
    heads = head_slices(2 * half_width)
    queries = [
        ref[:, head] for ref in (first_query_ref, last_query_ref) for head in head_slices(half_width)
    ]
    state = tuple(
        (stats_ref[0, h : h + 1, :], stats_ref[1, h : h + 1, :], summed_ref[head, :])
        for h, head in enumerate(heads)
    )
    for column, pair_ref, seg_ref in ((0, before_ref, before_seg_ref), (4, after_ref, after_seg_ref)):
        state = lax.fori_loop(
            bounds[block, column],
            bounds[block, column + 1],
            functools.partial(
                attend_step,
                [(pair_ref, head) for head in heads],
                seg_ref,
                query_seg_ref[...],
                queries,
            ),
            state,
        )
    rows = pl.ds(pl.multiple_of(block * QUERY_BLOCK, QUERY_BLOCK), QUERY_BLOCK)
    for head, (peak, total, summed) in zip(heads, state):
        attended_ref[rows, head] = (summed * (1.0 / total)).T.astype(jnp.bfloat16)

    @pl.when(block == pl.num_programs(0) - 1)
    def _():
        out_ref[...] = jnp.dot(
            place_ref[...], attended_ref[...], preferred_element_type=jnp.float32
        ).astype(jnp.bfloat16)


def whole(*shape):
    return pl.BlockSpec(shape, lambda i, b: (0,) * len(shape))


def at_column(shape, column):
    return pl.BlockSpec(shape, lambda i, b: (0,) * (len(shape) - 1) + (column,))


def query_rows(width, column):
    return pl.BlockSpec((QUERY_BLOCK, width), lambda i, b: (i, column))


def query_lanes(*shape):
    return pl.BlockSpec(shape + (QUERY_BLOCK,), lambda i, b: (0,) * len(shape) + (i,))


def attend_local(queries, pairs, quarters, query_seg, bounds):
    row_count, width = queries.shape
    quarter = width // 4
    head_count = width // (2 * HEAD)
    return pl.pallas_call(
        local_kernel,
        out_shape=(
            jax.ShapeDtypeStruct((2 * quarter, row_count), jnp.float32),
            jax.ShapeDtypeStruct((2, head_count, row_count), jnp.float32),
        ),
        grid_spec=pltpu.PrefetchScalarGridSpec(
            num_scalar_prefetch=1,
            grid=(row_count // QUERY_BLOCK,),
            in_specs=[query_rows(quarter, q) for q in quarters]
            + [at_column((2, row_count, quarter), q) for q in quarters]
            + [query_lanes(1), whole(row_count, 1)],
            out_specs=[query_lanes(2 * quarter), query_lanes(2, head_count)],
        ),
        compiler_params=pltpu.CompilerParams(vmem_limit_bytes=24 << 20),
        cost_estimate=pl.CostEstimate(
            flops=LOCAL_FLOPS_HINT, transcendentals=1 << 20, bytes_accessed=1 << 22
        ),
        name="attend_local",
    )(bounds, queries, queries, pairs, pairs, query_seg[None, :], query_seg[:, None])


def attend_halo(queries, halo, quarters, query_seg, margin_seg, bounds, local, placement):
    row_count, width = queries.shape
    quarter = width // 4
    head_count = width // (2 * HEAD)
    slot_count = placement.shape[0]
    return pl.pallas_call(
        halo_kernel,
        out_shape=jax.ShapeDtypeStruct((slot_count, 2 * quarter), jnp.bfloat16),
        grid_spec=pltpu.PrefetchScalarGridSpec(
            num_scalar_prefetch=1,
            grid=(row_count // QUERY_BLOCK,),
            in_specs=[query_rows(quarter, q) for q in quarters]
            + [whole(2, SEG_MAX, 2 * quarter)] * 2
            + [
                query_lanes(1),
                whole(SEG_MAX, 1),
                whole(SEG_MAX, 1),
                query_lanes(2 * quarter),
                query_lanes(2, head_count),
                whole(slot_count, row_count),
            ],
            out_specs=whole(slot_count, 2 * quarter),
            scratch_shapes=[pltpu.VMEM((row_count, 2 * quarter), jnp.bfloat16)],
        ),
        compiler_params=pltpu.CompilerParams(vmem_limit_bytes=24 << 20),
        cost_estimate=pl.CostEstimate(
            flops=HALO_FLOPS_HINT, transcendentals=1 << 20, bytes_accessed=1 << 22
        ),
        name="attend_halo",
    )(
        bounds, queries, queries, *halo, query_seg[None, :], margin_seg[:SEG_MAX, None],
        margin_seg[SEG_MAX + row_count :, None], *local, placement,
    )


def key_ranges(segment_ids, query_seg, first_row):
    row_count = query_seg.shape[0]
    firsts = query_seg[::QUERY_BLOCK]
    lasts = query_seg[QUERY_BLOCK - 1 :: QUERY_BLOCK]
    low = jnp.sum((segment_ids[None, :] < firsts[:, None]).astype(jnp.int32), axis=1)
    high = jnp.sum((segment_ids[None, :] <= lasts[:, None]).astype(jnp.int32), axis=1)
    columns = []
    for start, length in ((-SEG_MAX, SEG_MAX), (0, row_count), (row_count, SEG_MAX)):
        part_low = jnp.clip(low - first_row - start, 0, length)
        part_high = jnp.clip(high - first_row - start, 0, length)
        columns += [part_low // KEY_BLOCK, (part_high + KEY_BLOCK - 1) // KEY_BLOCK]
    return jnp.stack(columns, axis=1)


def body(
    queries, keys_values, segment_ids, route_shard, route_slot, control_proj, base_hidden, cotangent
):
    row_count = queries.shape[0]
    width = queries.shape[1]
    model_width = control_proj.shape[1]
    shard_count = lax.axis_size("seq")
    shard_index = lax.axis_index("seq")
    capacity = 2 * row_count // shard_count
    slot_count = shard_count * capacity
    block_rows = width // shard_count
    far_count = shard_count // 4
    core = shard_index % 2
    near = (shard_index // 2) % 2
    far = shard_index // 4
    quarter = width // 4
    far_quarter = far_count // 4

    def swap(value, bit):
        return lax.ppermute(value, "seq", [(i, i ^ bit) for i in range(shard_count)])

    def outer(value):
        return jnp.concatenate([value[..., :quarter], value[..., 3 * quarter :]], axis=-1)

    def inner(value):
        return value[..., quarter : 3 * quarter]

    up = [(i, i + 1) for i in range(shard_count - 1)]
    down = [(j, i) for i, j in up]

    def halo(pairs):
        before = lax.ppermute(pairs[:, row_count - SEG_MAX :], "seq", up)
        after = lax.ppermute(pairs[:, :SEG_MAX], "seq", down)
        return before, after

    first_halo = halo(outer(keys_values))
    gated, first_halo = lax.optimization_barrier((inner(keys_values), first_halo))
    second_halo = halo(gated)
    peer_cotangent = swap(cotangent, 1)

    target_shard = route_shard[:, 0]
    one_hot = (target_shard[:, None] == jnp.arange(shard_count, dtype=jnp.int32)[None, :]).astype(
        jnp.int32
    )
    slot_rank = jnp.sum((jnp.cumsum(one_hot, axis=0) - 1) * one_hot, axis=1)
    flat_place = target_shard * capacity + slot_rank
    place_mask = flat_place[None, :] == jnp.arange(slot_count, dtype=jnp.int32)[:, None]
    placement = place_mask.astype(jnp.bfloat16)
    occupied = jnp.sum(place_mask.astype(jnp.int32), axis=1)
    slot_values = jnp.sum(jnp.where(place_mask, route_slot[None, :], 0), axis=1)
    slot_table = jnp.where(occupied > 0, slot_values, -1).reshape(shard_count, capacity)
    incoming_slots = lax.all_to_all(slot_table, "seq", split_axis=0, concat_axis=0, tiled=True)
    landing = (
        incoming_slots.reshape(-1)[:, None] == jnp.arange(row_count, dtype=jnp.int32)[None, :]
    ).astype(jnp.bfloat16)

    first_row = shard_index * row_count
    query_seg = lax.dynamic_slice_in_dim(segment_ids, first_row, row_count)
    padded_seg = jnp.pad(segment_ids, (SEG_MAX, SEG_MAX), constant_values=-1)
    key_seg = lax.dynamic_slice_in_dim(padded_seg, first_row, row_count + 2 * SEG_MAX)
    bounds = key_ranges(segment_ids, query_seg, first_row)
    quarters = ((0, 3), (1, 2))
    outer_local = attend_local(queries, keys_values, quarters[0], query_seg, bounds)
    inner_local = attend_local(queries, keys_values, quarters[1], query_seg, bounds)
    outer_local, inner_local, first_halo = lax.optimization_barrier(
        (outer_local, inner_local, first_halo)
    )
    outer_placed = attend_halo(
        queries, first_halo, quarters[0], query_seg, key_seg, bounds, outer_local, placement
    )
    inner_placed = attend_halo(
        queries, second_halo, quarters[1], query_seg, key_seg, bounds, inner_local, placement
    )

    def split_columns(parts):
        step = model_width // parts
        return [slice(part * step, (part + 1) * step) for part in range(parts)]

    def product(halves, columns):
        return sum(
            jnp.einsum("fbt,td->fbd", half, other[:, columns], preferred_element_type=jnp.float32)
            for half, other in zip(halves, (cotangent, peer_cotangent))
        )

    def land(value):
        incoming = lax.all_to_all(
            value.reshape(shard_count, capacity, 2 * quarter),
            "seq",
            split_axis=0,
            concat_axis=0,
            tiled=True,
        )
        return jnp.einsum(
            "sk,sr->kr",
            incoming.reshape(slot_count, 2 * quarter),
            landing,
            preferred_element_type=jnp.float32,
        ).astype(jnp.bfloat16)

    def near_parts(rows):
        by_core = rows.reshape(far_count, 2, block_rows, row_count)
        peer_rows = swap(lax.dynamic_index_in_dim(by_core, 1 - core, 1, keepdims=False), 1)
        own_rows = lax.dynamic_index_in_dim(by_core, core, 1, keepdims=False)
        by_near = [
            value.reshape(far_count // 2, 2, block_rows, row_count) for value in (own_rows, peer_rows)
        ]
        return [
            [lax.dynamic_index_in_dim(v, which, 1, keepdims=False) for v in by_near]
            for which in (1 - near, near)
        ]

    def near_exchange(sent_rows, parts):
        sent = [product(sent_rows, columns).astype(jnp.bfloat16) for columns in split_columns(parts)]
        return sent, [swap(value, 2) for value in sent]

    def near_sum(kept_rows, arrived):
        return [
            product(kept_rows, columns) + value.astype(jnp.float32)
            for columns, value in zip(split_columns(len(arrived)), arrived)
        ]

    def line_exchange(chunk, summed, rounded):
        def pick(value, holder):
            return lax.dynamic_index_in_dim(
                value, jnp.where(far == holder, 1, 0), 0, keepdims=False
            )

        def hop(piece, moves):
            routes = [(4 * a + i, 4 * b + i) for a, b in moves for i in range(4)]
            return lax.ppermute(piece, "seq", routes)

        def add(holder, arrived):
            return (pick(summed, holder) + arrived.astype(jnp.float32)).astype(jnp.bfloat16)

        inward = hop(pick(rounded, 0), ((0, 1), (3, 2)))
        across = hop(add(1, inward), ((1, 2), (2, 1)))
        if chunk == 0:
            return [hop(add(2, across), ((2, 3), (1, 0)))]
        return [hop(pick(rounded, 3), ((0, 1), (3, 2))), across]

    def far_exchange(chunk, summed, rounded):
        members = [
            f for f in range(far_count) if (far_quarter <= f < 3 * far_quarter) == (chunk == 1)
        ]

        def place_of(index):
            if chunk == 1:
                return index - far_quarter
            return jnp.where(index < far_quarter, index, index - 2 * far_quarter)

        kept = lax.dynamic_index_in_dim(summed, place_of(far), 0, keepdims=False)
        if far_count == 4 and chunk == 1:
            return kept, line_exchange(chunk, summed, rounded)
        arrived = []
        for other in range(1, far_count):
            piece = lax.dynamic_index_in_dim(rounded, place_of(far ^ other), 0, keepdims=False)
            routes = [
                (i, i ^ (4 * other)) for i in range(shard_count) if (i // 4) ^ other in members
            ]
            arrived.append(lax.ppermute(piece, "seq", routes))
        return kept, arrived

    def far_total(kept, arrived):
        return kept + sum(value.astype(jnp.float32) for value in arrived)

    outer_rows = land(outer_placed)
    outer_sent_rows, outer_kept_rows = near_parts(outer_rows)
    outer_sent, outer_arrived = near_exchange(outer_sent_rows, OUTER_PARTS)
    early_rows, _ = lax.optimization_barrier((outer_rows, outer_sent))
    def project(rows, weights):
        return jnp.einsum("kr,kd->rd", rows, weights, preferred_element_type=jnp.float32)

    inner_weights = control_proj[quarter : 3 * quarter]
    early_mixed = (
        base_hidden.astype(jnp.float32)
        + project(early_rows[:quarter], control_proj[:quarter])
        + project(early_rows[quarter:], control_proj[3 * quarter :])
    )
    inner_rows = land(inner_placed)
    inner_sent_rows, inner_kept_rows = near_parts(inner_rows)
    inner_sent, inner_arrived = near_exchange(inner_sent_rows, INNER_PARTS)
    outer_arrived[1], _ = lax.optimization_barrier((outer_arrived[1], inner_rows))
    outer_arrived[0], early_mixed = lax.optimization_barrier((outer_arrived[0], early_mixed))
    outer_summed = near_sum(outer_kept_rows, outer_arrived)
    outer_far = [far_exchange(0, value, value.astype(jnp.bfloat16)) for value in outer_summed]
    inner_summed = near_sum(inner_kept_rows, inner_arrived)
    inner_rounded = [value.astype(jnp.bfloat16) for value in inner_summed]
    outer_far[0], _ = lax.optimization_barrier((outer_far[0], inner_sent))
    outer_far[1], _ = lax.optimization_barrier((outer_far[1], inner_rounded[0]))
    late_rows, _ = lax.optimization_barrier((inner_rows, inner_rounded[0]))
    inner_far = [far_exchange(1, *pair) for pair in zip(inner_summed, inner_rounded)]
    grad_parts = [
        jnp.concatenate([far_total(*pair) for pair in pairs], axis=1)
        for pairs in (outer_far, inner_far)
    ]
    in_middle = (far >= far_quarter) & (far < 3 * far_quarter)
    proj_grad = jnp.where(in_middle, grad_parts[1], grad_parts[0])

    mixed_hidden = (early_mixed + project(late_rows, inner_weights)).astype(jnp.bfloat16)
    return (mixed_hidden, proj_grad)


def solution(mesh):
    placed = (
        P(("grp", "seq"), None),
        P(None, ("grp", "seq"), None),
        P("grp"),
        P(("grp", "seq"), None),
        P(("grp", "seq")),
        P(),
        P(("grp", "seq"), None),
        P(("grp", "seq"), None),
    )
    return jax.shard_map(
        body,
        mesh=mesh,
        in_specs=placed,
        out_specs=(P(("grp", "seq"), None), P(("grp", "seq"), None)),
        check_vma=False,
    )
```
